512 devices in a mesh: segment: 8 (over y), rows: 64 (over x, z, core).
Axes of the slice: x: 4, y: 8, z: 8, core: 2. Of those that a mesh axis runs over, the one named last changes fastest.
Arguments:
- incoming: bfloat16 [8, 256, 128, 128], P('segment', 'rows'), may hold values from -6 to 6
- cotangent: bfloat16 [8, 256, 128, 128], P('segment', 'rows'), may hold values from -6 to 6
- main_weight: bfloat16 [8, 3, 3, 128, 128], P('segment'), may hold values from -0.1875 to 0.1875
- second_weight: bfloat16 [8, 3, 3, 128, 128], P('segment'), may hold values from -0.1875 to 0.1875
Outputs:
- output: bfloat16 [8, 256, 128, 128], P('segment', 'rows')
- input_grad: bfloat16 [8, 256, 128, 128], P('segment', 'rows')
- main_grad: float32 [8, 3, 3, 128, 128], P('segment')
- second_grad: float32 [8, 3, 3, 128, 128], P('segment')
The draws below stay inside these ranges and needn't reach their ends.
All inputs are finite; a program needn't handle non-finite values.
Results may differ from the reference program's by a relative error of at most 0.011.
Values may be sent and summed in bfloat16 or wider, within the bound.
A program may use at most 64 MiB of HBM per device.

```python
import math
import jax
import jax.numpy as jnp
from jax import lax

C = 128
W = 128
H = 256
N_SEGMENT = 8


def levels(rng, shape, shards, low, high):
    level = 1.0
    for axis_at, shards_of in shards:
        draws = jax.random.uniform(jax.random.fold_in(jax.random.fold_in(rng, 6), axis_at), (shards_of,), jnp.float32, low / len(shards), high / len(shards))
        level = level * jnp.repeat(jnp.exp(draws), shape[axis_at] // shards_of).reshape((-1,) + (1,) * (len(shape) - 1 - axis_at))
    return level


def scatter_about(stream_key, shape, scale, bound, split=(), kind=jnp.bfloat16):
    entries = jax.random.normal(stream_key, shape, jnp.float32) * scale
    if len(split) > 0:
        entries = levels(stream_key, shape, split, -0.22, 0.18) * entries
    return jnp.clip(entries, min=-bound, max=bound).astype(kind)


def setup_inputs(seed: int = 0) -> dict:
    seeds = jax.random.split(jax.random.key(seed), 5)
    return {
        "incoming": scatter_about(seeds[0], (N_SEGMENT, H, W, C), 1.0, 6.0, ((0, 8), (1, 64))),
        "cotangent": scatter_about(seeds[1], (N_SEGMENT, H, W, C), 1.0, 6.0, ((0, 8), (1, 64))),
        "main_weight": scatter_about(seeds[2], (N_SEGMENT, 3, 3, C, C), (9 * C) ** -0.5, 0.1875, ((0, 8),)),
        "second_weight": scatter_about(seeds[3], (N_SEGMENT, 3, 3, C, C), (9 * C) ** -0.5, 0.1875, ((0, 8),)),
    }


def silu(values):
    return values * jax.nn.sigmoid(values)

def slope(values):
    gate_value = jax.nn.sigmoid(values)
    return gate_value * (1.0 + values * (1.0 - gate_value))

def rimmed(field):
    return jnp.pad(field, ((1, 1), (0, 0), (0, 0)))

def widen(padded):
    breadth = padded.shape[1]
    widened = jnp.pad(padded, ((0, 0), (1, 1), (0, 0)))
    return jnp.concatenate([widened[:, 0:breadth], widened[:, 1:breadth + 1], widened[:, 2:breadth + 2]], axis=-1)

def convolve(padded, weight):
    stacked = widen(padded)
    height = padded.shape[0] - 2
    breadth = padded.shape[1]
    inner_dim = stacked.shape[-1]
    summed = jnp.zeros((height * breadth, weight.shape[-1]), jnp.float32)
    for offset in range(3):
        summed = summed + jnp.dot(stacked[offset:offset + height].reshape(-1, inner_dim), weight[offset].reshape(inner_dim, -1), preferred_element_type=jnp.float32)
    return summed.reshape(height, breadth, -1)

def transpose_conv(padded, weight):
    return convolve(padded, jnp.flip(weight, (0, 1)).transpose(0, 1, 3, 2))

def weight_grad(padded, gradient):
    stacked = widen(padded)
    height = gradient.shape[0]
    inner_dim = stacked.shape[-1]
    outer_dim = gradient.shape[-1]
    pieces = []
    for offset in range(3):
        product = lax.dot_general(stacked[offset:offset + height].reshape(-1, inner_dim), gradient.reshape(-1, outer_dim), (((0,), (0,)), ((), ())), preferred_element_type=jnp.float32)
        pieces.append(product.reshape(3, -1, outer_dim))
    return jnp.stack(pieces)

def reference(incoming, cotangent, main_weight, second_weight):
    segments = incoming.shape[0]
    factor = 1.0 / math.sqrt(H * W)
    outputs = [None] * segments
    inputs_back = [None] * segments
    firsts = [None] * segments
    seconds = [None] * segments
    for encoder_segment in range(segments // 2):
        decoder_segment = encoder_segment + segments // 2
        source_enc = incoming[encoder_segment]
        source_dec = incoming[decoder_segment]
        first_pre = convolve(rimmed(source_enc), main_weight[encoder_segment])
        hidden = silu(first_pre).astype(jnp.bfloat16)
        encoder_pre = convolve(rimmed(hidden), second_weight[encoder_segment])
        skip = silu(encoder_pre).astype(jnp.bfloat16)
        decoder_pre = convolve(rimmed(source_dec), main_weight[decoder_segment]) + convolve(rimmed(skip), second_weight[decoder_segment])
        outputs[encoder_segment] = skip
        outputs[decoder_segment] = silu(decoder_pre).astype(jnp.bfloat16)
        decoder_grad = (cotangent[decoder_segment].astype(jnp.float32) * slope(decoder_pre)).astype(jnp.bfloat16)
        skip_grad = transpose_conv(rimmed(decoder_grad), second_weight[decoder_segment]).astype(jnp.bfloat16)
        inputs_back[decoder_segment] = transpose_conv(rimmed(decoder_grad), main_weight[decoder_segment]).astype(jnp.bfloat16)
        firsts[decoder_segment] = weight_grad(rimmed(source_dec), decoder_grad) * factor
        seconds[decoder_segment] = weight_grad(rimmed(skip), decoder_grad) * factor
        encoder_grad = ((cotangent[encoder_segment].astype(jnp.float32) + skip_grad.astype(jnp.float32)) * slope(encoder_pre)).astype(jnp.bfloat16)
        hidden_grad = (transpose_conv(rimmed(encoder_grad), second_weight[encoder_segment]) * slope(first_pre)).astype(jnp.bfloat16)
        inputs_back[encoder_segment] = transpose_conv(rimmed(hidden_grad), main_weight[encoder_segment]).astype(jnp.bfloat16)
        firsts[encoder_segment] = weight_grad(rimmed(source_enc), hidden_grad) * factor
        seconds[encoder_segment] = weight_grad(rimmed(hidden), encoder_grad) * factor
    return (jnp.stack(outputs), jnp.stack(inputs_back), jnp.stack(firsts), jnp.stack(seconds))
```

```python
import functools
import math

import jax
import jax.numpy as jnp
from jax import lax
from jax.experimental import pallas as pl
from jax.experimental.pallas import tpu as pltpu
from jax.sharding import PartitionSpec as P

BF16 = jnp.bfloat16
F32 = jnp.float32
CORES = 2
Z_SIZE = 8
C = 128
W = 128
STRIP = 4


def silu(values):
    return values * jax.nn.sigmoid(values)


def slope(values):
    gate_value = jax.nn.sigmoid(values)
    return gate_value * (1.0 + values * (1.0 - gate_value))


def shifted(values, by):
    count = values.shape[0]
    column = lax.rem(lax.broadcasted_iota(jnp.int32, values.shape, 0), W)
    edge = 0 if by == 1 else W - 1
    return jnp.where(column == edge, 0.0, pltpu.roll(values, by % count, 0))


def conv_matrix(ref):
    return jnp.concatenate(
        [jnp.concatenate([ref[0, ty, tx] for tx in range(3)], axis=1) for ty in range(3)], axis=0
    )


def transpose_matrix(ref):
    return jnp.concatenate(
        [
            jnp.concatenate([ref[0, 2 - ty, 2 - tx] for ty in range(3)], axis=1)
            for tx in range(3)
        ],
        axis=0,
    )


def convolve(field, matrix, transposed):
    height = field.shape[0] - 2
    stacked = jnp.concatenate([field[t : t + height] for t in range(3)], axis=-1)
    products = lax.dot_general(
        stacked.reshape(height * W, 3 * C),
        matrix,
        (((1,), (1 if transposed else 0,)), ((), ())),
        preferred_element_type=F32,
    )
    return (
        shifted(products[:, :C], 1) + products[:, C : 2 * C] + shifted(products[:, 2 * C :], -1)
    )


def weight_grad(field, gradient, out_ref, index):
    flat = gradient.reshape(STRIP * W, C)
    wide = flat.astype(F32)
    stacked = jnp.concatenate(
        [shifted(wide, -1).astype(BF16), flat, shifted(wide, 1).astype(BF16)], axis=1
    )
    for ty in range(3):
        taps = lax.dot_general(
            field[ty : ty + STRIP].reshape(STRIP * W, C),
            stacked,
            (((0,), (0,)), ((), ())),
            preferred_element_type=F32,
        )
        for tx in range(3):
            out_ref[index, ty * 3 + tx] = taps[:, tx * C : (tx + 1) * C].astype(BF16)


def kernel(
    nx, nz, segments,
    x_ref, g_ref, a_ref, b_ref,
    out_ref, ig_ref, gs_ref,
    xpad, spad, gpad, hpad, dpad, fpre, epre, stage, back,
    mine, from_core, xsend, xrecv, flat_buf, zsend, zrecv, zout, zall, xout, xall, other,
    send, recv,
):
    seg = lax.axis_index("segment")
    row = lax.axis_index("rows")
    rows = nx * nz * CORES
    half = segments // 2
    core = lax.rem(row, CORES)
    z = lax.rem(row // CORES, nz)
    x = row // (CORES * nz)
    encoder = seg < half
    up = (seg, lax.rem(row + rows - 1, rows))
    down = (seg, lax.rem(row + 1, rows))
    across = (lax.rem(seg + half, segments), row)
    pair = (seg, row + 1 - 2 * core)
    first_row = row == 0
    last_row = row == rows - 1

    def x_peer(d):
        return (seg, (lax.rem(x + d, nx) * nz + z) * CORES + core)

    def z_peer(d):
        return (seg, (x * nz + lax.rem(z + d, nz)) * CORES + core)

    used = [0]

    def remote(src, dst, device):
        k = used[0]
        used[0] += 1
        return pltpu.make_async_remote_copy(
            src_ref=src, dst_ref=dst, send_sem=send.at[k], recv_sem=recv.at[k],
            device_id=device, device_id_type=pl.DeviceIdType.MESH,
        )

    partners = [up, down, across]
    partners += [x_peer(d) for d in range(1, nx)] + [z_peer(d) for d in range(1, nz)]
    barrier = pltpu.get_barrier_semaphore()
    for device in partners:
        pl.semaphore_signal(
            barrier, inc=1, device_id=device, device_id_type=pl.DeviceIdType.MESH
        )
    pl.semaphore_wait(barrier, len(partners))

    x_up = remote(x_ref.at[0, 0:2], xpad.at[6:8], up)
    x_down = remote(x_ref.at[0, 2:4], xpad.at[0:2], down)
    g_up = remote(g_ref.at[0, 0:1], gpad.at[5:6], up)
    g_down = remote(g_ref.at[0, 3:4], gpad.at[0:1], down)
    skip_copy = remote(stage, spad.at[2:6], across)
    back_copy = remote(stage, back, across)
    s_up = remote(spad.at[2:4], spad.at[6:8], up)
    s_down = remote(spad.at[4:6], spad.at[0:2], down)

    x_up.start()
    x_down.start()
    xpad[2:6] = x_ref[0]

    @pl.when(jnp.logical_not(encoder))
    def _():
        g_up.start()
        g_down.start()
        gpad[1:5] = g_ref[0]

    def clear(ref, width, top):
        @pl.when(first_row)
        def _():
            ref[0:width] = jnp.zeros((width, W, C), BF16)

        @pl.when(last_row)
        def _():
            ref[top - width : top] = jnp.zeros((width, W, C), BF16)

    x_up.wait()
    x_down.wait()
    clear(xpad, 2, 8)
    fpre[...] = convolve(xpad[...], conv_matrix(a_ref), False)

    @pl.when(encoder)
    def _():
        hpad[...] = silu(fpre[...]).astype(BF16).reshape(6, W, C)
        clear(hpad, 1, 6)
        epre[...] = convolve(hpad[...], conv_matrix(b_ref), False)
        skip = silu(epre[...]).astype(BF16).reshape(4, W, C)
        stage[...] = skip
        skip_copy.start()
        out_ref[0] = skip
        skip_copy.wait_send()
        back_copy.wait_recv()
        total = g_ref[0].astype(F32) + back[...].astype(F32)
        spad[2:6] = (total * slope(epre[...]).reshape(4, W, C)).astype(BF16)
        s_up.start()
        s_down.start()
        weight_grad(hpad[...], spad[2:6], mine, 1)
        s_up.wait()
        s_down.wait()
        clear(spad, 2, 8)
        hidden_back = convolve(spad[...], transpose_matrix(b_ref), True)
        dpad[...] = (hidden_back * slope(fpre[...])).astype(BF16).reshape(6, W, C)
        clear(dpad, 1, 6)

    @pl.when(jnp.logical_not(encoder))
    def _():
        skip_copy.wait_recv()
        s_up.start()
        s_down.start()
        g_up.wait()
        g_down.wait()
        s_up.wait()
        s_down.wait()
        clear(spad, 2, 8)
        fpre[...] += convolve(spad[...], conv_matrix(b_ref), False)
        pre = fpre[...]
        dpad[...] = (gpad[...].astype(F32) * slope(pre).reshape(6, W, C)).astype(BF16)
        clear(dpad, 1, 6)
        stage[...] = convolve(dpad[...], transpose_matrix(b_ref), True).astype(BF16).reshape(
            4, W, C
        )
        back_copy.start()
        out_ref[0] = silu(fpre[W : 5 * W]).astype(BF16).reshape(4, W, C)
        weight_grad(spad[1:7], dpad[1:5], mine, 1)
        back_copy.wait_send()

    weight_grad(xpad[1:7], dpad[1:5], mine, 0)

    swap = remote(mine.at[1 - core], from_core, pair)
    swap.start()
    ig_ref[0] = convolve(dpad[...], transpose_matrix(a_ref), True).astype(BF16).reshape(4, W, C)
    swap.wait()
    part = C // nx
    for k in range(nx):
        rows_k = slice(k * part, (k + 1) * part)
        xsend[k] = (mine[core, :, rows_k].astype(F32) + from_core[:, rows_k].astype(F32)).astype(
            BF16
        )

    copies = [
        remote(xsend.at[lax.rem(x + d, nx)], xrecv.at[d - 1], x_peer(d)) for d in range(1, nx)
    ]
    for copy in copies:
        copy.start()
    for copy in copies:
        copy.wait()
    total = xsend[x].astype(F32)
    for d in range(1, nx):
        total = total + xrecv[d - 1].astype(F32)
    flat_buf[...] = total.reshape(9 * part, C)
    chunk = 9 * part // nz
    for k in range(nz):
        zsend[k] = flat_buf[k * chunk : (k + 1) * chunk].astype(BF16)
    copies = [
        remote(zsend.at[lax.rem(z + d, nz)], zrecv.at[d - 1], z_peer(d)) for d in range(1, nz)
    ]
    for copy in copies:
        copy.start()
    for copy in copies:
        copy.wait()
    total = zsend[z].astype(F32)
    for d in range(1, nz):
        total = total + zrecv[d - 1].astype(F32)
    zout[...] = total.astype(BF16)

    copies = [remote(zout, zall.at[z], z_peer(d)) for d in range(1, nz)]
    for copy in copies:
        copy.start()
    zall[z] = zout[...]
    for copy in copies:
        copy.wait()
    for k in range(nz):
        flat_buf[k * chunk : (k + 1) * chunk] = zall[k].astype(F32)
    xout[...] = flat_buf[...].astype(BF16).reshape(9, part, C)
    copies = [remote(xout, xall.at[x], x_peer(d)) for d in range(1, nx)]
    for copy in copies:
        copy.start()
    forwards = [remote(xout, other.at[x], pair)]
    forwards[0].start()
    xall[x] = xout[...]
    for d in range(1, nx):
        copies[d - 1].wait()
        source = lax.rem(x + nx - d, nx)
        forwards.append(remote(xall.at[source], other.at[source], pair))
        forwards[d].start()
    for k in range(nx):
        gs_ref[core, :, k * part : (k + 1) * part] = xall[k]
    for copy in forwards:
        copy.wait()
    for k in range(nx):
        gs_ref[1 - core, :, k * part : (k + 1) * part] = other[k]


def body(nx, nz, segments, incoming, cotangent, main_weight, second_weight):
    part = C // nx
    chunk = 9 * part // nz
    field = (1, STRIP, W, C)
    copies = 9 + 2 * (nx - 1) + 2 * (nz - 1) + nx
    vmem = pl.BlockSpec(memory_space=pltpu.VMEM)
    output, input_grad, sums = pl.pallas_call(
        functools.partial(kernel, nx, nz, segments),
        out_shape=(
            jax.ShapeDtypeStruct(field, BF16),
            jax.ShapeDtypeStruct(field, BF16),
            jax.ShapeDtypeStruct((2, 9, C, C), BF16),
        ),
        in_specs=[vmem] * 4,
        out_specs=(vmem,) * 3,
        scratch_shapes=[
            pltpu.VMEM((8, W, C), BF16),
            pltpu.VMEM((8, W, C), BF16),
            pltpu.VMEM((6, W, C), BF16),
            pltpu.VMEM((6, W, C), BF16),
            pltpu.VMEM((6, W, C), BF16),
            pltpu.VMEM((6 * W, C), F32),
            pltpu.VMEM((4 * W, C), F32),
            pltpu.VMEM((4, W, C), BF16),
            pltpu.VMEM((4, W, C), BF16),
            pltpu.VMEM((2, 9, C, C), BF16),
            pltpu.VMEM((9, C, C), BF16),
            pltpu.VMEM((nx, 9, part, C), BF16),
            pltpu.VMEM((nx - 1, 9, part, C), BF16),
            pltpu.VMEM((9 * part, C), F32),
            pltpu.VMEM((nz, chunk, C), BF16),
            pltpu.VMEM((nz - 1, chunk, C), BF16),
            pltpu.VMEM((chunk, C), BF16),
            pltpu.VMEM((nz, chunk, C), BF16),
            pltpu.VMEM((9, part, C), BF16),
            pltpu.VMEM((nx, 9, part, C), BF16),
            pltpu.VMEM((nx, 9, part, C), BF16),
            pltpu.SemaphoreType.DMA((copies,)),
            pltpu.SemaphoreType.DMA((copies,)),
        ],
        compiler_params=pltpu.CompilerParams(
            collective_id=0, has_side_effects=True, vmem_limit_bytes=48 * 2**20
        ),
    )(incoming, cotangent, main_weight, second_weight)
    factor = 1.0 / math.sqrt(STRIP * nx * nz * CORES * W)
    grads = (sums.astype(F32) * factor).reshape(2, 1, 3, 3, C, C)
    return output, input_grad, grads[0], grads[1]


def build(mesh, nz):
    segments = mesh.shape["segment"]
    nx = mesh.shape["rows"] // (nz * CORES)
    field = P("segment", "rows", None, None)
    weight = P("segment", None, None, None, None)
    return jax.shard_map(
        functools.partial(body, nx, nz, segments),
        mesh=mesh,
        in_specs=(field, field, weight, weight),
        out_specs=(field, field, weight, weight),
        check_vma=False,
    )


def solution(mesh):
    return build(mesh, Z_SIZE)
```

```python
import functools
import math

import jax
import jax.numpy as jnp
from jax import lax
from jax.experimental import pallas as pl
from jax.experimental.pallas import tpu as pltpu
from jax.sharding import PartitionSpec as P

BF16 = jnp.bfloat16
F32 = jnp.float32
CORES = 2
Z_SIZE = 8
C = 128
W = 128
STRIP = 4
HALF = C // CORES
VMEM_BYTES = 67_043_328


def silu(values):
    return values * jax.nn.sigmoid(values)


def slope(values):
    gate_value = jax.nn.sigmoid(values)
    return gate_value * (1.0 + values * (1.0 - gate_value))


def shifted(values, by):
    count = values.shape[0]
    column = lax.rem(lax.broadcasted_iota(jnp.int32, values.shape, 0), W)
    edge = 0 if by == 1 else W - 1
    return jnp.where(column == edge, 0.0, pltpu.roll(values, by % count, 0))


def conv_matrix(ref):
    return jnp.concatenate(
        [jnp.concatenate([ref[0, ty, tx] for tx in range(3)], axis=1) for ty in range(3)], axis=0
    )


def transpose_matrix(ref):
    return jnp.concatenate(
        [
            jnp.concatenate([ref[0, 2 - ty, 2 - tx] for ty in range(3)], axis=1)
            for tx in range(3)
        ],
        axis=0,
    )


def convolve(field, matrix, transposed):
    height = field.shape[0] - 2
    stacked = jnp.concatenate([field[t : t + height] for t in range(3)], axis=-1)
    products = lax.dot_general(
        stacked.reshape(height * W, 3 * C),
        matrix,
        (((1,), (1 if transposed else 0,)), ((), ())),
        preferred_element_type=F32,
    )
    return (
        shifted(products[:, :C], 1) + products[:, C : 2 * C] + shifted(products[:, 2 * C :], -1)
    )


def weight_grad(field, gradient, out_ref, index):
    flat = gradient.reshape(STRIP * W, C)
    wide = flat.astype(F32)
    stacked = jnp.concatenate(
        [shifted(wide, -1).astype(BF16), flat, shifted(wide, 1).astype(BF16)], axis=1
    )
    for ty in range(3):
        taps = lax.dot_general(
            field[ty : ty + STRIP].reshape(STRIP * W, C),
            stacked,
            (((0,), (0,)), ((), ())),
            preferred_element_type=F32,
        )
        for tx in range(3):
            tap = taps[:, tx * C : (tx + 1) * C].astype(BF16)
            for core in range(CORES):
                out_ref[index, core, ty * 3 + tx] = tap[core * HALF : (core + 1) * HALF]


def kernel(
    nx, nz, segments,
    x_ref, g_ref, a_hbm, b_hbm,
    out_hbm, ig_hbm, gs_hbm,
    out_ref, ig_ref, gs_ref, xpad, spad, gpad, hpad, dpad, a_ref, b_ref, fpre, epre, stage, back,
    mine, from_core, xsend, xrecv, flat_buf, zsend, zrecv, zout, zall, xout, xall, other,
    local, send, recv,
):
    seg = lax.axis_index("segment")
    row = lax.axis_index("rows")
    rows = nx * nz * CORES
    half = segments // 2
    core = lax.rem(row, CORES)
    z = lax.rem(row // CORES, nz)
    x = row // (CORES * nz)
    encoder = seg < half
    up = (seg, lax.rem(row + rows - 1, rows))
    down = (seg, lax.rem(row + 1, rows))
    across = (lax.rem(seg + half, segments), row)
    pair = (seg, row + 1 - 2 * core)
    first_row = row == 0
    last_row = row == rows - 1

    def x_peer(d):
        return (seg, (lax.rem(x + d, nx) * nz + z) * CORES + core)

    def z_peer(d):
        return (seg, (x * nz + lax.rem(z + d, nz)) * CORES + core)

    used = [0]

    def remote(src, dst, device):
        k = used[0]
        used[0] += 1
        return pltpu.make_async_remote_copy(
            src_ref=src, dst_ref=dst, send_sem=send.at[k], recv_sem=recv.at[k],
            device_id=device, device_id_type=pl.DeviceIdType.MESH,
        )

    partners = [up, down, across]
    partners += [x_peer(d) for d in range(1, nx)] + [z_peer(d) for d in range(1, nz)]
    loads = [
        pltpu.make_async_copy(src, dst, local.at[k])
        for k, (src, dst) in enumerate(
            [
                (x_ref.at[0], xpad.at[2:6]),
                (a_hbm, a_ref),
                (g_ref.at[0], gpad.at[1:5]),
                (b_hbm, b_ref),
            ]
        )
    ]
    for load in loads:
        load.start()

    barrier = pltpu.get_barrier_semaphore()
    for device in partners:
        pl.semaphore_signal(
            barrier, inc=1, device_id=device, device_id_type=pl.DeviceIdType.MESH
        )
    pl.semaphore_wait(barrier, len(partners))

    x_up = remote(x_ref.at[0, 0:2], xpad.at[6:8], up)
    x_down = remote(x_ref.at[0, 2:4], xpad.at[0:2], down)
    g_up = remote(g_ref.at[0, 0:1], gpad.at[5:6], up)
    g_down = remote(g_ref.at[0, 3:4], gpad.at[0:1], down)
    skip_copy = remote(stage, spad.at[2:6], across)
    back_copy = remote(stage, back, across)
    s_up = remote(spad.at[2:4], spad.at[6:8], up)
    s_down = remote(spad.at[4:6], spad.at[0:2], down)

    part = HALF // nx
    chunk = 9 * part // nz

    class Reduction:
        def __init__(self, i):
            self.i = i
            self.pair = remote(mine.at[i, 1 - core], from_core.at[i], pair)
            self.x = [
                remote(xsend.at[i, lax.rem(x + d, nx)], xrecv.at[i, d - 1], x_peer(d))
                for d in range(1, nx)
            ]
            self.z = [
                remote(zsend.at[i, lax.rem(z + d, nz)], zrecv.at[i, d - 1], z_peer(d))
                for d in range(1, nz)
            ]
            self.z_back = [remote(zout.at[i], zall.at[i, z], z_peer(d)) for d in range(1, nz)]
            self.x_back = [remote(xout.at[i], xall.at[i, x], x_peer(d)) for d in range(1, nx)]
            self.over = [remote(xout.at[i], other.at[i, x], pair)]
            for d in range(1, nx):
                source = lax.rem(x + nx - d, nx)
                self.over.append(remote(xall.at[i, source], other.at[i, source], pair))

        def swap(self):
            self.pair.start()

        def reduce_x(self):
            i = self.i
            self.pair.wait()
            for k in range(nx):
                at = slice(k * part, (k + 1) * part)
                own = mine[i, core, :, at].astype(F32)
                xsend[i, k] = (own + from_core[i, :, at].astype(F32)).astype(BF16)
            for copy in self.x:
                copy.start()

        def reduce_z(self):
            i = self.i
            for copy in self.x:
                copy.wait()
            total = xsend[i, x].astype(F32)
            for d in range(1, nx):
                total = total + xrecv[i, d - 1].astype(F32)
            flat_buf[i] = total.reshape(9 * part, C)
            for k in range(nz):
                zsend[i, k] = flat_buf[i, k * chunk : (k + 1) * chunk].astype(BF16)
            for copy in self.z:
                copy.start()

        def gather_z(self):
            i = self.i
            for copy in self.z:
                copy.wait()
            total = zsend[i, z].astype(F32)
            for d in range(1, nz):
                total = total + zrecv[i, d - 1].astype(F32)
            zout[i] = total.astype(BF16)
            for copy in self.z_back:
                copy.start()
            zall[i, z] = zout[i]

        def gather_x(self):
            i = self.i
            for copy in self.z_back:
                copy.wait()
            for k in range(nz):
                flat_buf[i, k * chunk : (k + 1) * chunk] = zall[i, k].astype(F32)
            xout[i] = flat_buf[i].astype(BF16).reshape(9, part, C)
            for copy in self.x_back:
                copy.start()
            self.over[0].start()
            xall[i, x] = xout[i]

        def gather_core(self):
            for d in range(1, nx):
                self.x_back[d - 1].wait()
                self.over[d].start()

        def finish(self):
            i = self.i
            base = core * HALF
            for k in range(nx):
                at = pl.ds(pl.multiple_of(base + k * part, part), part)
                gs_ref[i, :, at] = xall[i, k]
            base = HALF - base
            for copy in self.over:
                copy.wait()
            for k in range(nx):
                at = pl.ds(pl.multiple_of(base + k * part, part), part)
                gs_ref[i, :, at] = other[i, k]

    first = Reduction(0)
    second = Reduction(1)

    x_up.start()
    x_down.start()

    @pl.when(jnp.logical_not(encoder))
    def _():
        g_up.start()
        g_down.start()

    def clear(ref, width, top):
        @pl.when(first_row)
        def _():
            ref[0:width] = jnp.zeros((width, W, C), BF16)

        @pl.when(last_row)
        def _():
            ref[top - width : top] = jnp.zeros((width, W, C), BF16)

    for load in loads:
        load.wait()
    x_up.wait()
    x_down.wait()
    clear(xpad, 2, 8)
    fpre[...] = convolve(xpad[...], conv_matrix(a_ref), False)

    @pl.when(encoder)
    def _():
        hpad[...] = silu(fpre[...]).astype(BF16).reshape(6, W, C)
        clear(hpad, 1, 6)
        epre[...] = convolve(hpad[...], conv_matrix(b_ref), False)
        skip = silu(epre[...]).astype(BF16).reshape(4, W, C)
        stage[...] = skip
        skip_copy.start()
        out_ref[...] = skip
        skip_copy.wait_send()
        back_copy.wait_recv()
        total = gpad[1:5].astype(F32) + back[...].astype(F32)
        spad[2:6] = (total * slope(epre[...]).reshape(4, W, C)).astype(BF16)
        s_up.start()
        s_down.start()
        weight_grad(hpad[...], spad[2:6], mine, 1)
        second.swap()
        s_up.wait()
        s_down.wait()
        clear(spad, 2, 8)
        second.reduce_x()
        hidden_back = convolve(spad[...], transpose_matrix(b_ref), True)
        dpad[...] = (hidden_back * slope(fpre[...])).astype(BF16).reshape(6, W, C)
        clear(dpad, 1, 6)

    @pl.when(jnp.logical_not(encoder))
    def _():
        skip_copy.wait_recv()
        s_up.start()
        s_down.start()
        g_up.wait()
        g_down.wait()
        s_up.wait()
        s_down.wait()
        clear(spad, 2, 8)
        fpre[...] += convolve(spad[...], conv_matrix(b_ref), False)
        pre = fpre[...]
        dpad[...] = (gpad[...].astype(F32) * slope(pre).reshape(6, W, C)).astype(BF16)
        clear(dpad, 1, 6)
        stage[...] = convolve(dpad[...], transpose_matrix(b_ref), True).astype(BF16).reshape(
            4, W, C
        )
        back_copy.start()
        out_ref[...] = silu(fpre[W : 5 * W]).astype(BF16).reshape(4, W, C)
        weight_grad(spad[1:7], dpad[1:5], mine, 1)
        second.swap()
        back_copy.wait_send()
        second.reduce_x()

    weight_grad(xpad[1:7], dpad[1:5], mine, 0)

    first.swap()
    second.reduce_z()
    store_out = pltpu.make_async_copy(out_ref, out_hbm.at[0], local.at[4])
    store_out.start()
    ig_ref[...] = convolve(dpad[...], transpose_matrix(a_ref), True).astype(BF16).reshape(4, W, C)
    store_ig = pltpu.make_async_copy(ig_ref, ig_hbm.at[0], local.at[5])
    store_ig.start()
    first.reduce_x()
    second.gather_z()
    first.reduce_z()
    second.gather_x()
    first.gather_z()
    second.gather_core()
    first.gather_x()
    first.gather_core()
    second.finish()
    store_second = pltpu.make_async_copy(gs_ref.at[1], gs_hbm.at[1], local.at[6])
    store_second.start()
    first.finish()
    store_first = pltpu.make_async_copy(gs_ref.at[0], gs_hbm.at[0], local.at[7])
    store_first.start()
    for store in (store_out, store_ig, store_second, store_first):
        store.wait()


def finish_kernel(
    factor, out_in, ig_in, gs_in, out_hbm, ig_hbm, first_hbm, second_hbm,
    out_ref, ig_ref, gs_ref, first, second, loaded, stored,
):
    loads = [
        pltpu.make_async_copy(src, dst, loaded.at[k])
        for k, (src, dst) in enumerate(
            [
                (gs_in.at[0], gs_ref.at[0]),
                (gs_in.at[1], gs_ref.at[1]),
                (out_in, out_ref),
                (ig_in, ig_ref),
            ]
        )
    ]
    stores = [
        pltpu.make_async_copy(src, dst, stored.at[k])
        for k, (src, dst) in enumerate(
            [(first, first_hbm), (second, second_hbm), (out_ref, out_hbm), (ig_ref, ig_hbm)]
        )
    ]
    for load in loads:
        load.start()
    for k, sums in enumerate((first, second)):
        loads[k].wait()
        sums[...] = (gs_ref[k].astype(F32) * factor).reshape(1, 3, 3, C, C)
        stores[k].start()
    for k in (2, 3):
        loads[k].wait()
        stores[k].start()
    for store in stores:
        store.wait()


def body(nx, nz, segments, incoming, cotangent, main_weight, second_weight):
    part = HALF // nx
    chunk = 9 * part // nz
    field = (1, STRIP, W, C)
    copies = 8 + 2 * (1 + 2 * (nx - 1) + 2 * (nz - 1) + nx)
    hbm = pl.BlockSpec(memory_space=pltpu.HBM)
    output, input_grad, sums = pl.pallas_call(
        functools.partial(kernel, nx, nz, segments),
        out_shape=(
            jax.ShapeDtypeStruct(field, BF16),
            jax.ShapeDtypeStruct(field, BF16),
            jax.ShapeDtypeStruct((2, 9, C, C), BF16),
        ),
        in_specs=[hbm] * 4,
        out_specs=(hbm,) * 3,
        scratch_shapes=[
            pltpu.VMEM((STRIP, W, C), BF16),
            pltpu.VMEM((STRIP, W, C), BF16),
            pltpu.VMEM((2, 9, C, C), BF16),
            pltpu.VMEM((8, W, C), BF16),
            pltpu.VMEM((8, W, C), BF16),
            pltpu.VMEM((6, W, C), BF16),
            pltpu.VMEM((6, W, C), BF16),
            pltpu.VMEM((6, W, C), BF16),
            pltpu.VMEM((1, 3, 3, C, C), BF16),
            pltpu.VMEM((1, 3, 3, C, C), BF16),
            pltpu.VMEM((6 * W, C), F32),
            pltpu.VMEM((4 * W, C), F32),
            pltpu.VMEM((4, W, C), BF16),
            pltpu.VMEM((4, W, C), BF16),
            pltpu.VMEM((2, CORES, 9, HALF, C), BF16),
            pltpu.VMEM((2, 9, HALF, C), BF16),
            pltpu.VMEM((2, nx, 9, part, C), BF16),
            pltpu.VMEM((2, nx - 1, 9, part, C), BF16),
            pltpu.VMEM((2, 9 * part, C), F32),
            pltpu.VMEM((2, nz, chunk, C), BF16),
            pltpu.VMEM((2, nz - 1, chunk, C), BF16),
            pltpu.VMEM((2, chunk, C), BF16),
            pltpu.VMEM((2, nz, chunk, C), BF16),
            pltpu.VMEM((2, 9, part, C), BF16),
            pltpu.VMEM((2, nx, 9, part, C), BF16),
            pltpu.VMEM((2, nx, 9, part, C), BF16),
            pltpu.SemaphoreType.DMA((8,)),
            pltpu.SemaphoreType.DMA((copies,)),
            pltpu.SemaphoreType.DMA((copies,)),
        ],
        compiler_params=pltpu.CompilerParams(
            collective_id=0, has_side_effects=True, vmem_limit_bytes=VMEM_BYTES
        ),
    )(incoming, cotangent, main_weight, second_weight)
    factor = 1.0 / math.sqrt(STRIP * nx * nz * CORES * W)
    weight = (1, 3, 3, C, C)
    return pl.pallas_call(
        functools.partial(finish_kernel, factor),
        out_shape=(
            jax.ShapeDtypeStruct(field, BF16),
            jax.ShapeDtypeStruct(field, BF16),
            jax.ShapeDtypeStruct(weight, F32),
            jax.ShapeDtypeStruct(weight, F32),
        ),
        in_specs=[hbm] * 3,
        out_specs=(hbm,) * 4,
        scratch_shapes=[
            pltpu.VMEM(field, BF16),
            pltpu.VMEM(field, BF16),
            pltpu.VMEM((2, 9, C, C), BF16),
            pltpu.VMEM(weight, F32),
            pltpu.VMEM(weight, F32),
            pltpu.SemaphoreType.DMA((4,)),
            pltpu.SemaphoreType.DMA((4,)),
        ],
        compiler_params=pltpu.CompilerParams(vmem_limit_bytes=VMEM_BYTES),
    )(output, input_grad, sums)


def build(mesh, nz):
    segments = mesh.shape["segment"]
    nx = mesh.shape["rows"] // (nz * CORES)
    field = P("segment", "rows", None, None)
    weight = P("segment", None, None, None, None)
    return jax.shard_map(
        functools.partial(body, nx, nz, segments),
        mesh=mesh,
        in_specs=(field, field, weight, weight),
        out_specs=(field, field, weight, weight),
        check_vma=False,
    )


def solution(mesh):
    return build(mesh, Z_SIZE)
```

```python
import functools
import math

import jax
import jax.numpy as jnp
from jax import lax
from jax.experimental import pallas as pl
from jax.experimental.pallas import tpu as pltpu
from jax.sharding import PartitionSpec as P

BF16 = jnp.bfloat16
F32 = jnp.float32
CORES = 2
Z_SIZE = 8
C = 128
W = 128
STRIP = 4
HALF = C // CORES
VMEM_BYTES = 67_043_328


def silu(values):
    return values * jax.nn.sigmoid(values)


def slope(values):
    gate_value = jax.nn.sigmoid(values)
    return gate_value * (1.0 + values * (1.0 - gate_value))


def shifted(values, by):
    count = values.shape[0]
    column = lax.rem(lax.broadcasted_iota(jnp.int32, values.shape, 0), W)
    edge = 0 if by == 1 else W - 1
    return jnp.where(column == edge, 0.0, pltpu.roll(values, by % count, 0))


def conv_matrix(ref):
    return jnp.concatenate(
        [jnp.concatenate([ref[0, ty, tx] for tx in range(3)], axis=1) for ty in range(3)], axis=0
    )


def transpose_matrix(ref):
    return jnp.concatenate(
        [
            jnp.concatenate([ref[0, 2 - ty, 2 - tx] for ty in range(3)], axis=1)
            for tx in range(3)
        ],
        axis=0,
    )


def convolve(field, matrix, transposed):
    height = field.shape[0] - 2
    stacked = jnp.concatenate([field[t : t + height] for t in range(3)], axis=-1)
    products = lax.dot_general(
        stacked.reshape(height * W, 3 * C),
        matrix,
        (((1,), (1 if transposed else 0,)), ((), ())),
        preferred_element_type=F32,
    )
    return (
        shifted(products[:, :C], 1) + products[:, C : 2 * C] + shifted(products[:, 2 * C :], -1)
    )


def weight_grad(field, gradient, out_ref, index):
    flat = gradient.reshape(STRIP * W, C)
    wide = flat.astype(F32)
    stacked = jnp.concatenate(
        [shifted(wide, -1).astype(BF16), flat, shifted(wide, 1).astype(BF16)], axis=1
    )
    for ty in range(3):
        taps = lax.dot_general(
            field[ty : ty + STRIP].reshape(STRIP * W, C),
            stacked,
            (((0,), (0,)), ((), ())),
            preferred_element_type=F32,
        )
        for tx in range(3):
            tap = taps[:, tx * C : (tx + 1) * C].astype(BF16)
            for core in range(CORES):
                out_ref[index, core, ty * 3 + tx] = tap[core * HALF : (core + 1) * HALF]


def kernel(
    nx, nz, segments,
    x_ref, g_ref, a_hbm, b_hbm,
    out_hbm, ig_hbm, gs_hbm,
    out_ref, ig_ref, gs_ref, xpad, spad, gpad, hpad, dpad, a_ref, b_ref, fpre, epre, stage, back,
    mine, from_core, xsend, xrecv, flat_buf, zsend, zrecv, zout, zall, xout, xall, other,
    local, send, recv,
):
    seg = lax.axis_index("segment")
    row = lax.axis_index("rows")
    rows = nx * nz * CORES
    half = segments // 2
    core = lax.rem(row, CORES)
    z = lax.rem(row // CORES, nz)
    x = row // (CORES * nz)
    encoder = seg < half
    up = (seg, lax.rem(row + rows - 1, rows))
    down = (seg, lax.rem(row + 1, rows))
    across = (lax.rem(seg + half, segments), row)
    pair = (seg, row + 1 - 2 * core)
    across_up = (across[0], up[1])
    across_down = (across[0], down[1])
    first_row = row == 0
    last_row = row == rows - 1

    def x_peer(d):
        return (seg, (lax.rem(x + d, nx) * nz + z) * CORES + core)

    def z_peer(d):
        return (seg, (x * nz + lax.rem(z + d, nz)) * CORES + core)

    used = [0]

    def remote(src, dst, device):
        k = used[0]
        used[0] += 1
        return pltpu.make_async_remote_copy(
            src_ref=src, dst_ref=dst, send_sem=send.at[k], recv_sem=recv.at[k],
            device_id=device, device_id_type=pl.DeviceIdType.MESH,
        )

    partners = [up, down, across, across_up, across_down]
    partners += [x_peer(d) for d in range(1, nx)] + [z_peer(d) for d in range(1, nz)]
    loads = [
        pltpu.make_async_copy(src, dst, local.at[k])
        for k, (src, dst) in enumerate(
            [
                (x_ref.at[0], xpad.at[2:6]),
                (a_hbm, a_ref),
                (g_ref.at[0], gpad.at[2:6]),
                (b_hbm, b_ref),
            ]
        )
    ]
    for load in loads:
        load.start()

    barrier = pltpu.get_barrier_semaphore()
    for device in partners:
        pl.semaphore_signal(
            barrier, inc=1, device_id=device, device_id_type=pl.DeviceIdType.MESH
        )
    pl.semaphore_wait(barrier, len(partners))

    x_up = remote(x_ref.at[0, 0:2], xpad.at[6:8], up)
    x_down = remote(x_ref.at[0, 2:4], xpad.at[0:2], down)
    g_up = remote(g_ref.at[0, 0:2], gpad.at[6:8], up)
    g_down = remote(g_ref.at[0, 2:4], gpad.at[0:2], down)
    e_up = remote(epre.at[2 * W : 4 * W], epre.at[6 * W : 8 * W], up)
    e_down = remote(epre.at[4 * W : 6 * W], epre.at[0 : 2 * W], down)

    def crossing(field):
        return (
            remote(stage, field.at[2:6], across),
            remote(stage.at[0:2], field.at[6:8], across_up),
            remote(stage.at[2:4], field.at[0:2], across_down),
        )

    skip_copies = crossing(spad)
    back_copies = crossing(back)

    part = HALF // nx
    chunk = 9 * part // nz

    class Reduction:
        def __init__(self, i):
            self.i = i
            self.pair = remote(mine.at[i, 1 - core], from_core.at[i], pair)
            self.x = [
                remote(xsend.at[i, lax.rem(x + d, nx)], xrecv.at[i, d - 1], x_peer(d))
                for d in range(1, nx)
            ]
            self.z = [
                remote(zsend.at[i, lax.rem(z + d, nz)], zrecv.at[i, d - 1], z_peer(d))
                for d in range(1, nz)
            ]
            self.z_back = [remote(zout.at[i], zall.at[i, z], z_peer(d)) for d in range(1, nz)]
            self.x_back = [remote(xout.at[i], xall.at[i, x], x_peer(d)) for d in range(1, nx)]
            self.over = [remote(xout.at[i], other.at[i, x], pair)]
            for d in range(1, nx):
                source = lax.rem(x + nx - d, nx)
                self.over.append(remote(xall.at[i, source], other.at[i, source], pair))

        def swap(self):
            self.pair.start()

        def reduce_x(self):
            i = self.i
            self.pair.wait()
            for k in range(nx):
                at = slice(k * part, (k + 1) * part)
                own = mine[i, core, :, at].astype(F32)
                xsend[i, k] = (own + from_core[i, :, at].astype(F32)).astype(BF16)
            for copy in self.x:
                copy.start()

        def reduce_z(self):
            i = self.i
            for copy in self.x:
                copy.wait()
            total = xsend[i, x].astype(F32)
            for d in range(1, nx):
                total = total + xrecv[i, d - 1].astype(F32)
            flat_buf[i] = total.reshape(9 * part, C)
            for k in range(nz):
                zsend[i, k] = flat_buf[i, k * chunk : (k + 1) * chunk].astype(BF16)
            for copy in self.z:
                copy.start()

        def gather_z(self):
            i = self.i
            for copy in self.z:
                copy.wait()
            total = zsend[i, z].astype(F32)
            for d in range(1, nz):
                total = total + zrecv[i, d - 1].astype(F32)
            zout[i] = total.astype(BF16)
            for copy in self.z_back:
                copy.start()
            zall[i, z] = zout[i]

        def gather_x(self):
            i = self.i
            for copy in self.z_back:
                copy.wait()
            for k in range(nz):
                flat_buf[i, k * chunk : (k + 1) * chunk] = zall[i, k].astype(F32)
            xout[i] = flat_buf[i].astype(BF16).reshape(9, part, C)
            for copy in self.x_back:
                copy.start()
            self.over[0].start()
            xall[i, x] = xout[i]

        def gather_core(self):
            for d in range(1, nx):
                self.x_back[d - 1].wait()
                self.over[d].start()

        def finish(self):
            i = self.i
            base = core * HALF
            for k in range(nx):
                at = pl.ds(pl.multiple_of(base + k * part, part), part)
                gs_ref[i, :, at] = xall[i, k]
            base = HALF - base
            for copy in self.over:
                copy.wait()
            for k in range(nx):
                at = pl.ds(pl.multiple_of(base + k * part, part), part)
                gs_ref[i, :, at] = other[i, k]

    first = Reduction(0)
    second = Reduction(1)

    x_up.start()
    x_down.start()

    g_up.start()
    g_down.start()

    def clear(ref, width, top):
        @pl.when(first_row)
        def _():
            ref[0:width] = jnp.zeros((width, W, C), BF16)

        @pl.when(last_row)
        def _():
            ref[top - width : top] = jnp.zeros((width, W, C), BF16)

    for load in loads:
        load.wait()
    x_up.wait()
    x_down.wait()
    clear(xpad, 2, 8)
    fpre[...] = convolve(xpad[...], conv_matrix(a_ref), False)

    @pl.when(encoder)
    def _():
        hpad[...] = silu(fpre[...]).astype(BF16).reshape(6, W, C)
        clear(hpad, 1, 6)
        epre[2 * W : 6 * W] = convolve(hpad[...], conv_matrix(b_ref), False)
        skip = silu(epre[2 * W : 6 * W]).astype(BF16).reshape(4, W, C)
        stage[...] = skip
        for copy in skip_copies:
            copy.start()
        e_up.start()
        e_down.start()
        out_ref[...] = skip
        g_up.wait()
        g_down.wait()
        e_up.wait()
        e_down.wait()
        for copy in skip_copies:
            copy.wait_send()
        epre[...] = slope(epre[...])
        for copy in back_copies:
            copy.wait_recv()
        total = gpad[...].astype(F32) + back[...].astype(F32)
        spad[...] = (total * epre[...].reshape(8, W, C)).astype(BF16)
        clear(spad, 2, 8)
        weight_grad(hpad[...], spad[2:6], mine, 1)
        second.swap()
        hidden_back = convolve(spad[...], transpose_matrix(b_ref), True)
        dpad[...] = (hidden_back * slope(fpre[...])).astype(BF16).reshape(6, W, C)
        clear(dpad, 1, 6)
        second.reduce_x()

    @pl.when(jnp.logical_not(encoder))
    def _():
        g_up.wait()
        g_down.wait()
        for copy in skip_copies:
            copy.wait_recv()
        clear(spad, 2, 8)
        fpre[...] += convolve(spad[...], conv_matrix(b_ref), False)
        pre = fpre[...]
        dpad[...] = (gpad[1:7].astype(F32) * slope(pre).reshape(6, W, C)).astype(BF16)
        clear(dpad, 1, 6)
        stage[...] = convolve(dpad[...], transpose_matrix(b_ref), True).astype(BF16).reshape(
            4, W, C
        )
        for copy in back_copies:
            copy.start()
        out_ref[...] = silu(fpre[W : 5 * W]).astype(BF16).reshape(4, W, C)
        weight_grad(spad[1:7], dpad[1:5], mine, 1)
        second.swap()
        for copy in back_copies:
            copy.wait_send()
        second.reduce_x()

    weight_grad(xpad[1:7], dpad[1:5], mine, 0)

    first.swap()
    second.reduce_z()
    store_out = pltpu.make_async_copy(out_ref, out_hbm.at[0], local.at[4])
    store_out.start()
    ig_ref[...] = convolve(dpad[...], transpose_matrix(a_ref), True).astype(BF16).reshape(4, W, C)
    store_ig = pltpu.make_async_copy(ig_ref, ig_hbm.at[0], local.at[5])
    store_ig.start()
    first.reduce_x()
    second.gather_z()
    first.reduce_z()
    second.gather_x()
    first.gather_z()
    second.gather_core()
    first.gather_x()
    first.gather_core()
    second.finish()
    store_second = pltpu.make_async_copy(gs_ref.at[1], gs_hbm.at[1], local.at[6])
    store_second.start()
    first.finish()
    store_first = pltpu.make_async_copy(gs_ref.at[0], gs_hbm.at[0], local.at[7])
    store_first.start()
    for store in (store_out, store_ig, store_second, store_first):
        store.wait()


def finish_kernel(
    factor, out_in, ig_in, gs_in, out_hbm, ig_hbm, first_hbm, second_hbm,
    out_ref, ig_ref, gs_ref, first, second, loaded, stored,
):
    loads = [
        pltpu.make_async_copy(src, dst, loaded.at[k])
        for k, (src, dst) in enumerate(
            [
                (gs_in.at[0], gs_ref.at[0]),
                (gs_in.at[1], gs_ref.at[1]),
                (out_in, out_ref),
                (ig_in, ig_ref),
            ]
        )
    ]
    stores = [
        pltpu.make_async_copy(src, dst, stored.at[k])
        for k, (src, dst) in enumerate(
            [(first, first_hbm), (second, second_hbm), (out_ref, out_hbm), (ig_ref, ig_hbm)]
        )
    ]
    for load in loads:
        load.start()
    for k, sums in enumerate((first, second)):
        loads[k].wait()
        sums[...] = (gs_ref[k].astype(F32) * factor).reshape(1, 3, 3, C, C)
        stores[k].start()
    for k in (2, 3):
        loads[k].wait()
        stores[k].start()
    for store in stores:
        store.wait()


def body(nx, nz, segments, incoming, cotangent, main_weight, second_weight):
    part = HALF // nx
    chunk = 9 * part // nz
    field = (1, STRIP, W, C)
    copies = 12 + 2 * (1 + 2 * (nx - 1) + 2 * (nz - 1) + nx)
    hbm = pl.BlockSpec(memory_space=pltpu.HBM)
    output, input_grad, sums = pl.pallas_call(
        functools.partial(kernel, nx, nz, segments),
        out_shape=(
            jax.ShapeDtypeStruct(field, BF16),
            jax.ShapeDtypeStruct(field, BF16),
            jax.ShapeDtypeStruct((2, 9, C, C), BF16),
        ),
        in_specs=[hbm] * 4,
        out_specs=(hbm,) * 3,
        scratch_shapes=[
            pltpu.VMEM((STRIP, W, C), BF16),
            pltpu.VMEM((STRIP, W, C), BF16),
            pltpu.VMEM((2, 9, C, C), BF16),
            pltpu.VMEM((8, W, C), BF16),
            pltpu.VMEM((8, W, C), BF16),
            pltpu.VMEM((8, W, C), BF16),
            pltpu.VMEM((6, W, C), BF16),
            pltpu.VMEM((6, W, C), BF16),
            pltpu.VMEM((1, 3, 3, C, C), BF16),
            pltpu.VMEM((1, 3, 3, C, C), BF16),
            pltpu.VMEM((6 * W, C), F32),
            pltpu.VMEM((8 * W, C), F32),
            pltpu.VMEM((4, W, C), BF16),
            pltpu.VMEM((8, W, C), BF16),
            pltpu.VMEM((2, CORES, 9, HALF, C), BF16),
            pltpu.VMEM((2, 9, HALF, C), BF16),
            pltpu.VMEM((2, nx, 9, part, C), BF16),
            pltpu.VMEM((2, nx - 1, 9, part, C), BF16),
            pltpu.VMEM((2, 9 * part, C), F32),
            pltpu.VMEM((2, nz, chunk, C), BF16),
            pltpu.VMEM((2, nz - 1, chunk, C), BF16),
            pltpu.VMEM((2, chunk, C), BF16),
            pltpu.VMEM((2, nz, chunk, C), BF16),
            pltpu.VMEM((2, 9, part, C), BF16),
            pltpu.VMEM((2, nx, 9, part, C), BF16),
            pltpu.VMEM((2, nx, 9, part, C), BF16),
            pltpu.SemaphoreType.DMA((8,)),
            pltpu.SemaphoreType.DMA((copies,)),
            pltpu.SemaphoreType.DMA((copies,)),
        ],
        compiler_params=pltpu.CompilerParams(
            collective_id=0, has_side_effects=True, vmem_limit_bytes=VMEM_BYTES
        ),
    )(incoming, cotangent, main_weight, second_weight)
    factor = 1.0 / math.sqrt(STRIP * nx * nz * CORES * W)
    weight = (1, 3, 3, C, C)
    return pl.pallas_call(
        functools.partial(finish_kernel, factor),
        out_shape=(
            jax.ShapeDtypeStruct(field, BF16),
            jax.ShapeDtypeStruct(field, BF16),
            jax.ShapeDtypeStruct(weight, F32),
            jax.ShapeDtypeStruct(weight, F32),
        ),
        in_specs=[hbm] * 3,
        out_specs=(hbm,) * 4,
        scratch_shapes=[
            pltpu.VMEM(field, BF16),
            pltpu.VMEM(field, BF16),
            pltpu.VMEM((2, 9, C, C), BF16),
            pltpu.VMEM(weight, F32),
            pltpu.VMEM(weight, F32),
            pltpu.SemaphoreType.DMA((4,)),
            pltpu.SemaphoreType.DMA((4,)),
        ],
        compiler_params=pltpu.CompilerParams(vmem_limit_bytes=VMEM_BYTES),
    )(output, input_grad, sums)


def build(mesh, nz):
    segments = mesh.shape["segment"]
    nx = mesh.shape["rows"] // (nz * CORES)
    field = P("segment", "rows", None, None)
    weight = P("segment", None, None, None, None)
    return jax.shard_map(
        functools.partial(body, nx, nz, segments),
        mesh=mesh,
        in_specs=(field, field, weight, weight),
        out_specs=(field, field, weight, weight),
        check_vma=False,
    )


def solution(mesh):
    return build(mesh, Z_SIZE)
```

```python
import functools
import math

import jax
import jax.numpy as jnp
from jax import lax
from jax.experimental import pallas as pl
from jax.experimental.pallas import tpu as pltpu
from jax.sharding import PartitionSpec as P

BF16 = jnp.bfloat16
F32 = jnp.float32
CORES = 2
Z_SIZE = 8
C = 128
W = 128
STRIP = 4
HALF = C // CORES
VMEM_BYTES = 67_043_328


def silu(values):
    return values * jax.nn.sigmoid(values)


def slope(values):
    gate_value = jax.nn.sigmoid(values)
    return gate_value * (1.0 + values * (1.0 - gate_value))


def shifted(values, by):
    count = values.shape[0]
    column = lax.rem(lax.broadcasted_iota(jnp.int32, values.shape, 0), W)
    edge = 0 if by == 1 else W - 1
    return jnp.where(column == edge, 0.0, pltpu.roll(values, by % count, 0))


def conv_matrix(ref):
    return jnp.concatenate(
        [jnp.concatenate([ref[0, ty, tx] for tx in range(3)], axis=1) for ty in range(3)], axis=0
    )


def transpose_matrix(ref):
    return jnp.concatenate(
        [
            jnp.concatenate([ref[0, 2 - ty, 2 - tx] for ty in range(3)], axis=1)
            for tx in range(3)
        ],
        axis=0,
    )


def convolve(field, matrix, transposed):
    height = field.shape[0] - 2
    stacked = jnp.concatenate([field[t : t + height] for t in range(3)], axis=-1)
    products = lax.dot_general(
        stacked.reshape(height * W, 3 * C),
        matrix,
        (((1,), (1 if transposed else 0,)), ((), ())),
        preferred_element_type=F32,
    )
    return (
        shifted(products[:, :C], 1) + products[:, C : 2 * C] + shifted(products[:, 2 * C :], -1)
    )


def weight_grad(field, gradient, out_ref, index):
    flat = gradient.reshape(STRIP * W, C)
    wide = flat.astype(F32)
    stacked = jnp.concatenate(
        [shifted(wide, -1).astype(BF16), flat, shifted(wide, 1).astype(BF16)], axis=1
    )
    for ty in range(3):
        taps = lax.dot_general(
            field[ty : ty + STRIP].reshape(STRIP * W, C),
            stacked,
            (((0,), (0,)), ((), ())),
            preferred_element_type=F32,
        )
        for tx in range(3):
            tap = taps[:, tx * C : (tx + 1) * C].astype(BF16)
            for core in range(CORES):
                out_ref[index, core, ty * 3 + tx] = tap[core * HALF : (core + 1) * HALF]


def kernel(
    nx, nz, segments,
    x_ref, g_ref, a_hbm, b_hbm,
    out_hbm, ig_hbm, gs_hbm,
    out_ref, ig_ref, gs_ref, xpad, spad, gpad, hpad, dpad, a_ref, b_ref, fpre, epre, stage, back,
    mine, from_core, xsend, xrecv, flat_buf, zsend, zrecv, zout, zall, xout, xall, other,
    local, send, recv,
):
    seg = lax.axis_index("segment")
    row = lax.axis_index("rows")
    rows = nx * nz * CORES
    half = segments // 2
    core = lax.rem(row, CORES)
    z = lax.rem(row // CORES, nz)
    x = row // (CORES * nz)
    encoder = seg < half
    up = (seg, lax.rem(row + rows - 1, rows))
    down = (seg, lax.rem(row + 1, rows))
    across = (lax.rem(seg + half, segments), row)
    pair = (seg, row + 1 - 2 * core)
    first_row = row == 0
    last_row = row == rows - 1

    def x_peer(d):
        return (seg, (lax.rem(x + d, nx) * nz + z) * CORES + core)

    def z_peer(d):
        return (seg, (x * nz + lax.rem(z + d, nz)) * CORES + core)

    used = [0]

    class Rim:
        def __init__(self, up_copy, down_copy):
            self.up = up_copy
            self.down = down_copy

        def start_up(self):
            pl.when(jnp.logical_not(first_row))(self.up.start)

        def start_down(self):
            pl.when(jnp.logical_not(last_row))(self.down.start)

        def wait(self):
            @pl.when(jnp.logical_not(first_row))
            def _():
                self.up.wait_send()
                self.down.wait_recv()

            @pl.when(jnp.logical_not(last_row))
            def _():
                self.down.wait_send()
                self.up.wait_recv()

    def remote(src, dst, device):
        k = used[0]
        used[0] += 1
        return pltpu.make_async_remote_copy(
            src_ref=src, dst_ref=dst, send_sem=send.at[k], recv_sem=recv.at[k],
            device_id=device, device_id_type=pl.DeviceIdType.MESH,
        )

    partners = [up, down, across]
    partners += [x_peer(d) for d in range(1, nx)] + [z_peer(d) for d in range(1, nz)]
    loads = [
        pltpu.make_async_copy(src, dst, local.at[k])
        for k, (src, dst) in enumerate(
            [
                (x_ref.at[0], xpad.at[2:6]),
                (a_hbm, a_ref),
                (g_ref.at[0], gpad.at[1:5]),
                (b_hbm, b_ref),
            ]
        )
    ]
    for load in loads:
        load.start()

    barrier = pltpu.get_barrier_semaphore()
    for device in partners:
        pl.semaphore_signal(
            barrier, inc=1, device_id=device, device_id_type=pl.DeviceIdType.MESH
        )
    pl.semaphore_wait(barrier, len(partners))

    x_rim = Rim(
        remote(x_ref.at[0, 0:2], xpad.at[6:8], up), remote(x_ref.at[0, 2:4], xpad.at[0:2], down)
    )
    g_rim = Rim(
        remote(g_ref.at[0, 0:1], gpad.at[5:6], up), remote(g_ref.at[0, 3:4], gpad.at[0:1], down)
    )
    s_rim = Rim(
        remote(spad.at[2:4], spad.at[6:8], up), remote(spad.at[4:6], spad.at[0:2], down)
    )
    skip_copies = [
        remote(stage.at[h : h + 2], spad.at[h + 2 : h + 4], across) for h in (0, 2)
    ]
    back_copies = [remote(stage.at[h : h + 2], back.at[h : h + 2], across) for h in (0, 2)]

    part = HALF // nx
    chunk = 9 * part // nz

    class Reduction:
        def __init__(self, i):
            self.i = i
            self.pair = remote(mine.at[i, 1 - core], from_core.at[i], pair)
            self.x = [
                remote(xsend.at[i, lax.rem(x + d, nx)], xrecv.at[i, d - 1], x_peer(d))
                for d in range(1, nx)
            ]
            self.z = [
                remote(zsend.at[i, lax.rem(z + d, nz)], zrecv.at[i, d - 1], z_peer(d))
                for d in range(1, nz)
            ]
            self.z_back = [remote(zout.at[i], zall.at[i, z], z_peer(d)) for d in range(1, nz)]
            self.x_back = [remote(xout.at[i], xall.at[i, x], x_peer(d)) for d in range(1, nx)]
            self.over = [remote(xout.at[i], other.at[i, x], pair)]
            for d in range(1, nx):
                source = lax.rem(x + nx - d, nx)
                self.over.append(remote(xall.at[i, source], other.at[i, source], pair))

        def swap(self):
            self.pair.start()

        def reduce_x(self):
            i = self.i
            self.pair.wait()
            for k in range(nx):
                at = slice(k * part, (k + 1) * part)
                own = mine[i, core, :, at].astype(F32)
                xsend[i, k] = (own + from_core[i, :, at].astype(F32)).astype(BF16)
            for copy in self.x:
                copy.start()

        def reduce_z(self):
            i = self.i
            for copy in self.x:
                copy.wait()
            total = xsend[i, x].astype(F32)
            for d in range(1, nx):
                total = total + xrecv[i, d - 1].astype(F32)
            flat_buf[i] = total.reshape(9 * part, C)
            for k in range(nz):
                zsend[i, k] = flat_buf[i, k * chunk : (k + 1) * chunk].astype(BF16)
            for copy in self.z:
                copy.start()

        def gather_z(self):
            i = self.i
            for copy in self.z:
                copy.wait()
            total = zsend[i, z].astype(F32)
            for d in range(1, nz):
                total = total + zrecv[i, d - 1].astype(F32)
            zout[i] = total.astype(BF16)
            for copy in self.z_back:
                copy.start()
            zall[i, z] = zout[i]

        def gather_x(self):
            i = self.i
            for copy in self.z_back:
                copy.wait()
            for k in range(nz):
                flat_buf[i, k * chunk : (k + 1) * chunk] = zall[i, k].astype(F32)
            xout[i] = flat_buf[i].astype(BF16).reshape(9, part, C)
            for copy in self.x_back:
                copy.start()
            self.over[0].start()
            xall[i, x] = xout[i]

        def gather_core(self):
            for d in range(1, nx):
                self.x_back[d - 1].wait()
                self.over[d].start()

        def finish(self):
            i = self.i
            base = core * HALF
            for k in range(nx):
                at = pl.ds(pl.multiple_of(base + k * part, part), part)
                gs_ref[i, :, at] = xall[i, k]
            base = HALF - base
            for copy in self.over:
                copy.wait()
            for k in range(nx):
                at = pl.ds(pl.multiple_of(base + k * part, part), part)
                gs_ref[i, :, at] = other[i, k]

    first = Reduction(0)
    second = Reduction(1)

    x_rim.start_up()
    x_rim.start_down()

    @pl.when(jnp.logical_not(encoder))
    def _():
        g_rim.start_up()
        g_rim.start_down()

    def clear(ref, width, top):
        @pl.when(first_row)
        def _():
            ref[0:width] = jnp.zeros((width, W, C), BF16)

        @pl.when(last_row)
        def _():
            ref[top - width : top] = jnp.zeros((width, W, C), BF16)

    for load in loads:
        load.wait()
    x_rim.wait()
    clear(xpad, 2, 8)
    fpre[...] = convolve(xpad[...], conv_matrix(a_ref), False)

    @pl.when(encoder)
    def _():
        hpad[...] = silu(fpre[...]).astype(BF16).reshape(6, W, C)
        clear(hpad, 1, 6)
        matrix = conv_matrix(b_ref)
        for h in (0, 2):
            pre = convolve(hpad[h : h + 4], matrix, False)
            stage[h : h + 2] = silu(pre).astype(BF16).reshape(2, W, C)
            skip_copies[h // 2].start()
            epre[h * W : (h + 2) * W] = pre
        out_ref[...] = stage[...]
        for copy in skip_copies:
            copy.wait_send()
        for copy in back_copies:
            copy.wait_recv()
        total = gpad[1:5].astype(F32) + back[...].astype(F32)
        spad[2:6] = (total * slope(epre[...]).reshape(4, W, C)).astype(BF16)
        s_rim.start_up()
        s_rim.start_down()
        weight_grad(hpad[...], spad[2:6], mine, 1)
        second.swap()
        s_rim.wait()
        clear(spad, 2, 8)
        second.reduce_x()
        hidden_back = convolve(spad[...], transpose_matrix(b_ref), True)
        dpad[...] = (hidden_back * slope(fpre[...])).astype(BF16).reshape(6, W, C)
        clear(dpad, 1, 6)

    @pl.when(jnp.logical_not(encoder))
    def _():
        skip_copies[0].wait_recv()
        s_rim.start_up()
        skip_copies[1].wait_recv()
        s_rim.start_down()
        g_rim.wait()
        s_rim.wait()
        clear(spad, 2, 8)
        fpre[...] += convolve(spad[...], conv_matrix(b_ref), False)
        pre = fpre[...]
        dpad[...] = (gpad[...].astype(F32) * slope(pre).reshape(6, W, C)).astype(BF16)
        clear(dpad, 1, 6)
        matrix = transpose_matrix(b_ref)
        for h in (0, 2):
            skip_grad = convolve(dpad[h : h + 4], matrix, True)
            stage[h : h + 2] = skip_grad.astype(BF16).reshape(2, W, C)
            back_copies[h // 2].start()
        out_ref[...] = silu(fpre[W : 5 * W]).astype(BF16).reshape(4, W, C)
        weight_grad(spad[1:7], dpad[1:5], mine, 1)
        second.swap()
        for copy in back_copies:
            copy.wait_send()
        second.reduce_x()

    weight_grad(xpad[1:7], dpad[1:5], mine, 0)

    first.swap()
    second.reduce_z()
    store_out = pltpu.make_async_copy(out_ref, out_hbm.at[0], local.at[4])
    store_out.start()
    ig_ref[...] = convolve(dpad[...], transpose_matrix(a_ref), True).astype(BF16).reshape(4, W, C)
    store_ig = pltpu.make_async_copy(ig_ref, ig_hbm.at[0], local.at[5])
    store_ig.start()
    first.reduce_x()
    second.gather_z()
    first.reduce_z()
    second.gather_x()
    first.gather_z()
    second.gather_core()
    first.gather_x()
    first.gather_core()
    second.finish()
    store_second = pltpu.make_async_copy(gs_ref.at[1], gs_hbm.at[1], local.at[6])
    store_second.start()
    first.finish()
    store_first = pltpu.make_async_copy(gs_ref.at[0], gs_hbm.at[0], local.at[7])
    store_first.start()
    for store in (store_out, store_ig, store_second, store_first):
        store.wait()


def finish_kernel(
    factor, out_in, ig_in, gs_in, out_hbm, ig_hbm, first_hbm, second_hbm,
    out_ref, ig_ref, gs_ref, first, second, loaded, stored,
):
    loads = [
        pltpu.make_async_copy(src, dst, loaded.at[k])
        for k, (src, dst) in enumerate(
            [
                (gs_in.at[0], gs_ref.at[0]),
                (gs_in.at[1], gs_ref.at[1]),
                (out_in, out_ref),
                (ig_in, ig_ref),
            ]
        )
    ]
    stores = [
        pltpu.make_async_copy(src, dst, stored.at[k])
        for k, (src, dst) in enumerate(
            [(first, first_hbm), (second, second_hbm), (out_ref, out_hbm), (ig_ref, ig_hbm)]
        )
    ]
    for load in loads:
        load.start()
    for k, sums in enumerate((first, second)):
        loads[k].wait()
        sums[...] = (gs_ref[k].astype(F32) * factor).reshape(1, 3, 3, C, C)
        stores[k].start()
    for k in (2, 3):
        loads[k].wait()
        stores[k].start()
    for store in stores:
        store.wait()


def body(nx, nz, segments, incoming, cotangent, main_weight, second_weight):
    part = HALF // nx
    chunk = 9 * part // nz
    field = (1, STRIP, W, C)
    copies = 10 + 2 * (1 + 2 * (nx - 1) + 2 * (nz - 1) + nx)
    hbm = pl.BlockSpec(memory_space=pltpu.HBM)
    output, input_grad, sums = pl.pallas_call(
        functools.partial(kernel, nx, nz, segments),
        out_shape=(
            jax.ShapeDtypeStruct(field, BF16),
            jax.ShapeDtypeStruct(field, BF16),
            jax.ShapeDtypeStruct((2, 9, C, C), BF16),
        ),
        in_specs=[hbm] * 4,
        out_specs=(hbm,) * 3,
        scratch_shapes=[
            pltpu.VMEM((STRIP, W, C), BF16),
            pltpu.VMEM((STRIP, W, C), BF16),
            pltpu.VMEM((2, 9, C, C), BF16),
            pltpu.VMEM((8, W, C), BF16),
            pltpu.VMEM((8, W, C), BF16),
            pltpu.VMEM((6, W, C), BF16),
            pltpu.VMEM((6, W, C), BF16),
            pltpu.VMEM((6, W, C), BF16),
            pltpu.VMEM((1, 3, 3, C, C), BF16),
            pltpu.VMEM((1, 3, 3, C, C), BF16),
            pltpu.VMEM((6 * W, C), F32),
            pltpu.VMEM((4 * W, C), F32),
            pltpu.VMEM((4, W, C), BF16),
            pltpu.VMEM((4, W, C), BF16),
            pltpu.VMEM((2, CORES, 9, HALF, C), BF16),
            pltpu.VMEM((2, 9, HALF, C), BF16),
            pltpu.VMEM((2, nx, 9, part, C), BF16),
            pltpu.VMEM((2, nx - 1, 9, part, C), BF16),
            pltpu.VMEM((2, 9 * part, C), F32),
            pltpu.VMEM((2, nz, chunk, C), BF16),
            pltpu.VMEM((2, nz - 1, chunk, C), BF16),
            pltpu.VMEM((2, chunk, C), BF16),
            pltpu.VMEM((2, nz, chunk, C), BF16),
            pltpu.VMEM((2, 9, part, C), BF16),
            pltpu.VMEM((2, nx, 9, part, C), BF16),
            pltpu.VMEM((2, nx, 9, part, C), BF16),
            pltpu.SemaphoreType.DMA((8,)),
            pltpu.SemaphoreType.DMA((copies,)),
            pltpu.SemaphoreType.DMA((copies,)),
        ],
        compiler_params=pltpu.CompilerParams(
            collective_id=0, has_side_effects=True, vmem_limit_bytes=VMEM_BYTES
        ),
    )(incoming, cotangent, main_weight, second_weight)
    factor = 1.0 / math.sqrt(STRIP * nx * nz * CORES * W)
    weight = (1, 3, 3, C, C)
    return pl.pallas_call(
        functools.partial(finish_kernel, factor),
        out_shape=(
            jax.ShapeDtypeStruct(field, BF16),
            jax.ShapeDtypeStruct(field, BF16),
            jax.ShapeDtypeStruct(weight, F32),
            jax.ShapeDtypeStruct(weight, F32),
        ),
        in_specs=[hbm] * 3,
        out_specs=(hbm,) * 4,
        scratch_shapes=[
            pltpu.VMEM(field, BF16),
            pltpu.VMEM(field, BF16),
            pltpu.VMEM((2, 9, C, C), BF16),
            pltpu.VMEM(weight, F32),
            pltpu.VMEM(weight, F32),
            pltpu.SemaphoreType.DMA((4,)),
            pltpu.SemaphoreType.DMA((4,)),
        ],
        compiler_params=pltpu.CompilerParams(vmem_limit_bytes=VMEM_BYTES),
    )(output, input_grad, sums)


def build(mesh, nz):
    segments = mesh.shape["segment"]
    nx = mesh.shape["rows"] // (nz * CORES)
    field = P("segment", "rows", None, None)
    weight = P("segment", None, None, None, None)
    return jax.shard_map(
        functools.partial(body, nx, nz, segments),
        mesh=mesh,
        in_specs=(field, field, weight, weight),
        out_specs=(field, field, weight, weight),
        check_vma=False,
    )


def solution(mesh):
    return build(mesh, Z_SIZE)
```

```python
import functools
import math

import jax
import jax.numpy as jnp
from jax import lax
from jax.experimental import pallas as pl
from jax.experimental.pallas import tpu as pltpu
from jax.sharding import PartitionSpec as P

BF16 = jnp.bfloat16
F32 = jnp.float32
CORES = 2
Z_SIZE = 8
C = 128
W = 128
STRIP = 4
HALF = C // CORES
VMEM_BYTES = 67_043_328


def silu(values):
    return values * jax.nn.sigmoid(values)


def slope(values):
    gate_value = jax.nn.sigmoid(values)
    return gate_value * (1.0 + values * (1.0 - gate_value))


def shifted(values, by):
    count = values.shape[0]
    column = lax.rem(lax.broadcasted_iota(jnp.int32, values.shape, 0), W)
    edge = 0 if by == 1 else W - 1
    return jnp.where(column == edge, 0.0, pltpu.roll(values, by % count, 0))


def conv_matrix(ref):
    return jnp.concatenate(
        [jnp.concatenate([ref[0, ty, tx] for tx in range(3)], axis=1) for ty in range(3)], axis=0
    )


def transpose_matrix(ref):
    return jnp.concatenate(
        [
            jnp.concatenate([ref[0, 2 - ty, 2 - tx] for ty in range(3)], axis=1)
            for tx in range(3)
        ],
        axis=0,
    )


def convolve(field, matrix, transposed):
    height = field.shape[0] - 2
    stacked = jnp.concatenate([field[t : t + height] for t in range(3)], axis=-1)
    products = lax.dot_general(
        stacked.reshape(height * W, 3 * C),
        matrix,
        (((1,), (1 if transposed else 0,)), ((), ())),
        preferred_element_type=F32,
    )
    return (
        shifted(products[:, :C], 1) + products[:, C : 2 * C] + shifted(products[:, 2 * C :], -1)
    )


def weight_grad(field, gradient, out_ref, index):
    flat = gradient.reshape(STRIP * W, C)
    wide = flat.astype(F32)
    stacked = jnp.concatenate(
        [shifted(wide, -1).astype(BF16), flat, shifted(wide, 1).astype(BF16)], axis=1
    )
    for ty in range(3):
        taps = lax.dot_general(
            field[ty : ty + STRIP].reshape(STRIP * W, C),
            stacked,
            (((0,), (0,)), ((), ())),
            preferred_element_type=F32,
        )
        for tx in range(3):
            tap = taps[:, tx * C : (tx + 1) * C].astype(BF16)
            for core in range(CORES):
                out_ref[index, core, ty * 3 + tx] = tap[core * HALF : (core + 1) * HALF]


def kernel(
    nx, nz, segments,
    x_ref, g_ref, a_hbm, b_hbm,
    out_hbm, ig_hbm, gs_hbm,
    out_ref, ig_ref, gs_ref, xpad, spad, gpad, hpad, dpad, a_ref, b_ref, fpre, epre, stage, back,
    mine, from_core, xsend, xrecv, flat_buf, zsend, zrecv, zout, zall, xout, xall, other,
    local, send, recv,
):
    seg = lax.axis_index("segment")
    row = lax.axis_index("rows")
    rows = nx * nz * CORES
    half = segments // 2
    core = lax.rem(row, CORES)
    z = lax.rem(row // CORES, nz)
    x = row // (CORES * nz)
    encoder = seg < half
    up = (seg, lax.rem(row + rows - 1, rows))
    down = (seg, lax.rem(row + 1, rows))
    across = (lax.rem(seg + half, segments), row)
    pair = (seg, row + 1 - 2 * core)
    first_row = row == 0
    last_row = row == rows - 1

    def x_peer(d):
        return (seg, (lax.rem(x + d, nx) * nz + z) * CORES + core)

    def z_peer(d):
        return (seg, (x * nz + lax.rem(z + d, nz)) * CORES + core)

    used = [0]

    class Rim:
        def __init__(self, up_copy, down_copy):
            self.up = up_copy
            self.down = down_copy

        def start_up(self):
            pl.when(jnp.logical_not(first_row))(self.up.start)

        def start_down(self):
            pl.when(jnp.logical_not(last_row))(self.down.start)

        def wait(self):
            @pl.when(jnp.logical_not(first_row))
            def _():
                self.up.wait_send()
                self.down.wait_recv()

            @pl.when(jnp.logical_not(last_row))
            def _():
                self.down.wait_send()
                self.up.wait_recv()

    def remote(src, dst, device):
        k = used[0]
        used[0] += 1
        return pltpu.make_async_remote_copy(
            src_ref=src, dst_ref=dst, send_sem=send.at[k], recv_sem=recv.at[k],
            device_id=device, device_id_type=pl.DeviceIdType.MESH,
        )

    partners = [up, down, across]
    partners += [x_peer(d) for d in range(1, nx)] + [z_peer(d) for d in range(1, nz)]
    loads = [
        pltpu.make_async_copy(src, dst, local.at[k])
        for k, (src, dst) in enumerate(
            [
                (x_ref.at[0], xpad.at[2:6]),
                (a_hbm, a_ref),
                (g_ref.at[0], gpad.at[1:5]),
                (b_hbm, b_ref),
            ]
        )
    ]
    for load in loads:
        load.start()

    barrier = pltpu.get_barrier_semaphore()
    for device in partners:
        pl.semaphore_signal(
            barrier, inc=1, device_id=device, device_id_type=pl.DeviceIdType.MESH
        )
    pl.semaphore_wait(barrier, len(partners))

    x_rim = Rim(
        remote(x_ref.at[0, 0:2], xpad.at[6:8], up), remote(x_ref.at[0, 2:4], xpad.at[0:2], down)
    )
    g_rim = Rim(
        remote(g_ref.at[0, 0:1], gpad.at[5:6], up), remote(g_ref.at[0, 3:4], gpad.at[0:1], down)
    )
    s_rim = Rim(
        remote(spad.at[2:4], spad.at[6:8], up), remote(spad.at[4:6], spad.at[0:2], down)
    )
    skip_copies = [
        remote(stage.at[h : h + 2], spad.at[h + 2 : h + 4], across) for h in (0, 2)
    ]
    back_copies = [remote(stage.at[h : h + 2], back.at[h : h + 2], across) for h in (0, 2)]

    part = HALF // nx
    chunk = 9 * part // nz

    class Reduction:
        def __init__(self, i):
            self.i = i
            self.pair = remote(mine.at[i, 1 - core], from_core.at[i], pair)
            self.x = [
                remote(xsend.at[i, lax.rem(x + d, nx)], xrecv.at[i, d - 1], x_peer(d))
                for d in range(1, nx)
            ]
            self.z = [
                remote(zsend.at[i, lax.rem(z + d, nz)], zrecv.at[i, d - 1], z_peer(d))
                for d in range(1, nz)
            ]
            self.z_back = [remote(zout.at[i], zall.at[i, z], z_peer(d)) for d in range(1, nz)]
            self.x_back = [remote(xout.at[i], xall.at[i, x], x_peer(d)) for d in range(1, nx)]
            self.over = [remote(xout.at[i], other.at[i, x], pair)]
            for d in range(1, nx):
                source = lax.rem(x + nx - d, nx)
                self.over.append(remote(xall.at[i, source], other.at[i, source], pair))

        def swap(self):
            self.pair.start()

        def reduce_x(self):
            i = self.i
            self.pair.wait()
            for k in range(nx):
                at = slice(k * part, (k + 1) * part)
                own = mine[i, core, :, at].astype(F32)
                xsend[i, k] = (own + from_core[i, :, at].astype(F32)).astype(BF16)
            for copy in self.x:
                copy.start()

        def reduce_z(self):
            i = self.i
            for copy in self.x:
                copy.wait()
            total = xsend[i, x].astype(F32)
            for d in range(1, nx):
                total = total + xrecv[i, d - 1].astype(F32)
            flat_buf[i] = total.reshape(9 * part, C)
            for k in range(nz):
                zsend[i, k] = flat_buf[i, k * chunk : (k + 1) * chunk].astype(BF16)
            for copy in self.z:
                copy.start()

        def gather_z(self):
            i = self.i
            for copy in self.z:
                copy.wait()
            total = zsend[i, z].astype(F32)
            for d in range(1, nz):
                total = total + zrecv[i, d - 1].astype(F32)
            zout[i] = total.astype(BF16)
            for copy in self.z_back:
                copy.start()
            zall[i, z] = zout[i]

        def gather_x(self):
            i = self.i
            for copy in self.z_back:
                copy.wait()
            for k in range(nz):
                flat_buf[i, k * chunk : (k + 1) * chunk] = zall[i, k].astype(F32)
            xout[i] = flat_buf[i].astype(BF16).reshape(9, part, C)
            for copy in self.x_back:
                copy.start()
            self.over[0].start()
            xall[i, x] = xout[i]

        def gather_core(self):
            for d in range(1, nx):
                self.x_back[d - 1].wait()
                self.over[d].start()

        def finish(self):
            i = self.i
            base = core * HALF
            for k in range(nx):
                at = pl.ds(pl.multiple_of(base + k * part, part), part)
                gs_ref[i, :, at] = xall[i, k]
            base = HALF - base
            for copy in self.over:
                copy.wait()
            for k in range(nx):
                at = pl.ds(pl.multiple_of(base + k * part, part), part)
                gs_ref[i, :, at] = other[i, k]

    first = Reduction(0)
    second = Reduction(1)

    x_rim.start_up()
    x_rim.start_down()

    @pl.when(jnp.logical_not(encoder))
    def _():
        g_rim.start_up()
        g_rim.start_down()

    def clear(ref, width, top):
        @pl.when(first_row)
        def _():
            ref[0:width] = jnp.zeros((width, W, C), BF16)

        @pl.when(last_row)
        def _():
            ref[top - width : top] = jnp.zeros((width, W, C), BF16)

    for load in loads:
        load.wait()
    x_rim.wait()
    clear(xpad, 2, 8)
    fpre[...] = convolve(xpad[...], conv_matrix(a_ref), False)

    @pl.when(encoder)
    def _():
        hpad[...] = silu(fpre[...]).astype(BF16).reshape(6, W, C)
        clear(hpad, 1, 6)
        matrix = conv_matrix(b_ref)
        for h in (0, 2):
            pre = convolve(hpad[h : h + 4], matrix, False)
            stage[h : h + 2] = silu(pre).astype(BF16).reshape(2, W, C)
            skip_copies[h // 2].start()
            epre[h * W : (h + 2) * W] = pre
        out_ref[...] = stage[...]
        for copy in skip_copies:
            copy.wait_send()
        for copy in back_copies:
            copy.wait_recv()
        total = gpad[1:5].astype(F32) + back[...].astype(F32)
        spad[2:6] = (total * slope(epre[...]).reshape(4, W, C)).astype(BF16)
        s_rim.start_up()
        s_rim.start_down()
        weight_grad(hpad[...], spad[2:6], mine, 1)
        second.swap()
        s_rim.wait()
        clear(spad, 2, 8)
        second.reduce_x()
        hidden_back = convolve(spad[...], transpose_matrix(b_ref), True)
        dpad[...] = (hidden_back * slope(fpre[...])).astype(BF16).reshape(6, W, C)
        clear(dpad, 1, 6)

    @pl.when(jnp.logical_not(encoder))
    def _():
        skip_copies[0].wait_recv()
        s_rim.start_up()
        skip_copies[1].wait_recv()
        s_rim.start_down()
        g_rim.wait()
        s_rim.wait()
        clear(spad, 2, 8)
        fpre[...] += convolve(spad[...], conv_matrix(b_ref), False)
        pre = fpre[...]
        dpad[...] = (gpad[...].astype(F32) * slope(pre).reshape(6, W, C)).astype(BF16)
        clear(dpad, 1, 6)
        matrix = transpose_matrix(b_ref)
        for h in (0, 2):
            skip_grad = convolve(dpad[h : h + 4], matrix, True)
            stage[h : h + 2] = skip_grad.astype(BF16).reshape(2, W, C)
            back_copies[h // 2].start()
        out_ref[...] = silu(fpre[W : 5 * W]).astype(BF16).reshape(4, W, C)
        weight_grad(spad[1:7], dpad[1:5], mine, 1)
        second.swap()
        for copy in back_copies:
            copy.wait_send()
        second.reduce_x()

    weight_grad(xpad[1:7], dpad[1:5], mine, 0)

    first.swap()
    second.reduce_z()
    first.reduce_x()
    store_out = pltpu.make_async_copy(out_ref, out_hbm.at[0], local.at[4])
    store_out.start()
    ig_ref[...] = convolve(dpad[...], transpose_matrix(a_ref), True).astype(BF16).reshape(4, W, C)
    store_ig = pltpu.make_async_copy(ig_ref, ig_hbm.at[0], local.at[5])
    store_ig.start()
    first.reduce_z()
    second.gather_z()
    first.gather_z()
    second.gather_x()
    first.gather_x()
    second.gather_core()
    first.gather_core()
    second.finish()
    store_second = pltpu.make_async_copy(gs_ref.at[1], gs_hbm.at[1], local.at[6])
    store_second.start()
    first.finish()
    store_first = pltpu.make_async_copy(gs_ref.at[0], gs_hbm.at[0], local.at[7])
    store_first.start()
    for store in (store_out, store_ig, store_second, store_first):
        store.wait()


def finish_kernel(
    factor, out_in, ig_in, gs_in, out_hbm, ig_hbm, first_hbm, second_hbm,
    out_ref, ig_ref, gs_ref, first, second, loaded, stored,
):
    loads = [
        pltpu.make_async_copy(src, dst, loaded.at[k])
        for k, (src, dst) in enumerate(
            [
                (gs_in.at[0], gs_ref.at[0]),
                (gs_in.at[1], gs_ref.at[1]),
                (out_in, out_ref),
                (ig_in, ig_ref),
            ]
        )
    ]
    stores = [
        pltpu.make_async_copy(src, dst, stored.at[k])
        for k, (src, dst) in enumerate(
            [(first, first_hbm), (second, second_hbm), (out_ref, out_hbm), (ig_ref, ig_hbm)]
        )
    ]
    for load in loads:
        load.start()
    for k, sums in enumerate((first, second)):
        loads[k].wait()
        sums[...] = (gs_ref[k].astype(F32) * factor).reshape(1, 3, 3, C, C)
        stores[k].start()
    for k in (2, 3):
        loads[k].wait()
        stores[k].start()
    for store in stores:
        store.wait()


def body(nx, nz, segments, incoming, cotangent, main_weight, second_weight):
    part = HALF // nx
    chunk = 9 * part // nz
    field = (1, STRIP, W, C)
    copies = 10 + 2 * (1 + 2 * (nx - 1) + 2 * (nz - 1) + nx)
    hbm = pl.BlockSpec(memory_space=pltpu.HBM)
    output, input_grad, sums = pl.pallas_call(
        functools.partial(kernel, nx, nz, segments),
        out_shape=(
            jax.ShapeDtypeStruct(field, BF16),
            jax.ShapeDtypeStruct(field, BF16),
            jax.ShapeDtypeStruct((2, 9, C, C), BF16),
        ),
        in_specs=[hbm] * 4,
        out_specs=(hbm,) * 3,
        scratch_shapes=[
            pltpu.VMEM((STRIP, W, C), BF16),
            pltpu.VMEM((STRIP, W, C), BF16),
            pltpu.VMEM((2, 9, C, C), BF16),
            pltpu.VMEM((8, W, C), BF16),
            pltpu.VMEM((8, W, C), BF16),
            pltpu.VMEM((6, W, C), BF16),
            pltpu.VMEM((6, W, C), BF16),
            pltpu.VMEM((6, W, C), BF16),
            pltpu.VMEM((1, 3, 3, C, C), BF16),
            pltpu.VMEM((1, 3, 3, C, C), BF16),
            pltpu.VMEM((6 * W, C), F32),
            pltpu.VMEM((4 * W, C), F32),
            pltpu.VMEM((4, W, C), BF16),
            pltpu.VMEM((4, W, C), BF16),
            pltpu.VMEM((2, CORES, 9, HALF, C), BF16),
            pltpu.VMEM((2, 9, HALF, C), BF16),
            pltpu.VMEM((2, nx, 9, part, C), BF16),
            pltpu.VMEM((2, nx - 1, 9, part, C), BF16),
            pltpu.VMEM((2, 9 * part, C), F32),
            pltpu.VMEM((2, nz, chunk, C), BF16),
            pltpu.VMEM((2, nz - 1, chunk, C), BF16),
            pltpu.VMEM((2, chunk, C), BF16),
            pltpu.VMEM((2, nz, chunk, C), BF16),
            pltpu.VMEM((2, 9, part, C), BF16),
            pltpu.VMEM((2, nx, 9, part, C), BF16),
            pltpu.VMEM((2, nx, 9, part, C), BF16),
            pltpu.SemaphoreType.DMA((8,)),
            pltpu.SemaphoreType.DMA((copies,)),
            pltpu.SemaphoreType.DMA((copies,)),
        ],
        compiler_params=pltpu.CompilerParams(
            collective_id=0, has_side_effects=True, vmem_limit_bytes=VMEM_BYTES
        ),
    )(incoming, cotangent, main_weight, second_weight)
    factor = 1.0 / math.sqrt(STRIP * nx * nz * CORES * W)
    weight = (1, 3, 3, C, C)
    return pl.pallas_call(
        functools.partial(finish_kernel, factor),
        out_shape=(
            jax.ShapeDtypeStruct(field, BF16),
            jax.ShapeDtypeStruct(field, BF16),
            jax.ShapeDtypeStruct(weight, F32),
            jax.ShapeDtypeStruct(weight, F32),
        ),
        in_specs=[hbm] * 3,
        out_specs=(hbm,) * 4,
        scratch_shapes=[
            pltpu.VMEM(field, BF16),
            pltpu.VMEM(field, BF16),
            pltpu.VMEM((2, 9, C, C), BF16),
            pltpu.VMEM(weight, F32),
            pltpu.VMEM(weight, F32),
            pltpu.SemaphoreType.DMA((4,)),
            pltpu.SemaphoreType.DMA((4,)),
        ],
        compiler_params=pltpu.CompilerParams(vmem_limit_bytes=VMEM_BYTES),
    )(output, input_grad, sums)


def build(mesh, nz):
    segments = mesh.shape["segment"]
    nx = mesh.shape["rows"] // (nz * CORES)
    field = P("segment", "rows", None, None)
    weight = P("segment", None, None, None, None)
    return jax.shard_map(
        functools.partial(body, nx, nz, segments),
        mesh=mesh,
        in_specs=(field, field, weight, weight),
        out_specs=(field, field, weight, weight),
        check_vma=False,
    )


def solution(mesh):
    return build(mesh, Z_SIZE)
```

```python
import functools
import math

import jax
import jax.numpy as jnp
from jax import lax
from jax.experimental import pallas as pl
from jax.experimental.pallas import tpu as pltpu
from jax.sharding import PartitionSpec as P

BF16 = jnp.bfloat16
F32 = jnp.float32
CORES = 2
Z_SIZE = 8
C = 128
W = 128
STRIP = 4
HALF = C // CORES
VMEM_BYTES = 67_043_328


def silu(values):
    return values * jax.nn.sigmoid(values)


def slope(values):
    gate_value = jax.nn.sigmoid(values)
    return gate_value * (1.0 + values * (1.0 - gate_value))


def shifted(values, by):
    count = values.shape[0]
    column = lax.rem(lax.broadcasted_iota(jnp.int32, values.shape, 0), W)
    edge = 0 if by == 1 else W - 1
    return jnp.where(column == edge, 0.0, pltpu.roll(values, by % count, 0))


def conv_matrix(ref):
    return jnp.concatenate(
        [jnp.concatenate([ref[0, ty, tx] for tx in range(3)], axis=1) for ty in range(3)], axis=0
    )


def transpose_matrix(ref):
    return jnp.concatenate(
        [
            jnp.concatenate([ref[0, 2 - ty, 2 - tx] for ty in range(3)], axis=1)
            for tx in range(3)
        ],
        axis=0,
    )


def convolve(field, matrix, transposed):
    height = field.shape[0] - 2
    stacked = jnp.concatenate([field[t : t + height] for t in range(3)], axis=-1)
    products = lax.dot_general(
        stacked.reshape(height * W, 3 * C),
        matrix,
        (((1,), (1 if transposed else 0,)), ((), ())),
        preferred_element_type=F32,
    )
    return (
        shifted(products[:, :C], 1) + products[:, C : 2 * C] + shifted(products[:, 2 * C :], -1)
    )


def weight_grad(field, gradient, out_ref, index):
    flat = gradient.reshape(STRIP * W, C)
    wide = flat.astype(F32)
    stacked = jnp.concatenate(
        [shifted(wide, -1).astype(BF16), flat, shifted(wide, 1).astype(BF16)], axis=1
    )
    for ty in range(3):
        taps = lax.dot_general(
            field[ty : ty + STRIP].reshape(STRIP * W, C),
            stacked,
            (((0,), (0,)), ((), ())),
            preferred_element_type=F32,
        )
        for tx in range(3):
            tap = taps[:, tx * C : (tx + 1) * C].astype(BF16)
            for core in range(CORES):
                out_ref[index, core, ty * 3 + tx] = tap[core * HALF : (core + 1) * HALF]


def kernel(
    nx, nz, segments,
    x_ref, g_ref, a_hbm, b_hbm,
    out_hbm, ig_hbm, gs_hbm,
    out_ref, ig_ref, gs_ref, xpad, spad, gpad, hpad, dpad, a_ref, b_ref, fpre, epre, stage, back,
    mine, from_core, xsend, xrecv, flat_buf, zsend, zrecv, zout, zall, xout, xall, other,
    local, send, recv,
):
    seg = lax.axis_index("segment")
    row = lax.axis_index("rows")
    rows = nx * nz * CORES
    half = segments // 2
    core = lax.rem(row, CORES)
    z = lax.rem(row // CORES, nz)
    x = row // (CORES * nz)
    encoder = seg < half
    up = (seg, lax.rem(row + rows - 1, rows))
    down = (seg, lax.rem(row + 1, rows))
    across = (lax.rem(seg + half, segments), row)
    pair = (seg, row + 1 - 2 * core)
    first_row = row == 0
    last_row = row == rows - 1

    def x_peer(d):
        return (seg, (lax.rem(x + d, nx) * nz + z) * CORES + core)

    def z_peer(d):
        return (seg, (x * nz + lax.rem(z + d, nz)) * CORES + core)

    used = [0]

    class Rim:
        def __init__(self, up_copy, down_copy):
            self.up = up_copy
            self.down = down_copy

        def start_up(self):
            pl.when(jnp.logical_not(first_row))(self.up.start)

        def start_down(self):
            pl.when(jnp.logical_not(last_row))(self.down.start)

        def wait(self):
            @pl.when(jnp.logical_not(first_row))
            def _():
                self.up.wait_send()
                self.down.wait_recv()

            @pl.when(jnp.logical_not(last_row))
            def _():
                self.down.wait_send()
                self.up.wait_recv()

    def remote(src, dst, device):
        k = used[0]
        used[0] += 1
        return pltpu.make_async_remote_copy(
            src_ref=src, dst_ref=dst, send_sem=send.at[k], recv_sem=recv.at[k],
            device_id=device, device_id_type=pl.DeviceIdType.MESH,
        )

    partners = [up, down, across]
    partners += [x_peer(d) for d in range(1, nx)] + [z_peer(d) for d in range(1, nz)]
    loads = [
        pltpu.make_async_copy(src, dst, local.at[k])
        for k, (src, dst) in enumerate(
            [
                (x_ref.at[0], xpad.at[2:6]),
                (a_hbm, a_ref),
                (g_ref.at[0], gpad.at[1:5]),
                (b_hbm, b_ref),
            ]
        )
    ]
    for load in loads:
        load.start()

    barrier = pltpu.get_barrier_semaphore()
    for device in partners:
        pl.semaphore_signal(
            barrier, inc=1, device_id=device, device_id_type=pl.DeviceIdType.MESH
        )
    pl.semaphore_wait(barrier, len(partners))

    x_rim = Rim(
        remote(x_ref.at[0, 0:2], xpad.at[6:8], up), remote(x_ref.at[0, 2:4], xpad.at[0:2], down)
    )
    g_rim = Rim(
        remote(g_ref.at[0, 0:1], gpad.at[5:6], up), remote(g_ref.at[0, 3:4], gpad.at[0:1], down)
    )
    s_rim = Rim(
        remote(spad.at[2:4], spad.at[6:8], up), remote(spad.at[4:6], spad.at[0:2], down)
    )
    skip_copies = [
        remote(stage.at[h : h + 2], spad.at[h + 2 : h + 4], across) for h in (0, 2)
    ]
    back_copies = [remote(stage.at[h : h + 2], back.at[h : h + 2], across) for h in (0, 2)]

    part = HALF // nx
    chunk = 9 * part // nz

    class Reduction:
        def __init__(self, i):
            self.i = i
            self.pair = remote(mine.at[i, 1 - core], from_core.at[i], pair)
            self.x = [
                remote(xsend.at[i, lax.rem(x + d, nx)], xrecv.at[i, d - 1], x_peer(d))
                for d in range(1, nx)
            ]
            self.z = [
                remote(zsend.at[i, lax.rem(z + d, nz)], zrecv.at[i, d - 1], z_peer(d))
                for d in range(1, nz)
            ]
            self.z_back = [remote(zout.at[i], zall.at[i, z], z_peer(d)) for d in range(1, nz)]
            self.x_back = [remote(xout.at[i], xall.at[i, x], x_peer(d)) for d in range(1, nx)]
            self.over = [remote(xout.at[i], other.at[i, x], pair)]
            for d in range(1, nx):
                source = lax.rem(x + nx - d, nx)
                self.over.append(remote(xall.at[i, source], other.at[i, source], pair))

        def swap(self):
            self.pair.start()

        def reduce_x(self):
            i = self.i
            self.pair.wait()
            for k in range(nx):
                at = slice(k * part, (k + 1) * part)
                own = mine[i, core, :, at].astype(F32)
                xsend[i, k] = (own + from_core[i, :, at].astype(F32)).astype(BF16)
            for copy in farthest_first(self.x):
                copy.start()

        def reduce_z(self):
            i = self.i
            for copy in self.x:
                copy.wait()
            total = xsend[i, x].astype(F32)
            for d in range(1, nx):
                total = total + xrecv[i, d - 1].astype(F32)
            flat_buf[i] = total.reshape(9 * part, C)
            for k in range(nz):
                zsend[i, k] = flat_buf[i, k * chunk : (k + 1) * chunk].astype(BF16)
            for copy in farthest_first(self.z):
                copy.start()

        def gather_z(self):
            i = self.i
            for copy in self.z:
                copy.wait()
            total = zsend[i, z].astype(F32)
            for d in range(1, nz):
                total = total + zrecv[i, d - 1].astype(F32)
            zout[i] = total.astype(BF16)
            for copy in farthest_first(self.z_back):
                copy.start()
            zall[i, z] = zout[i]

        def gather_x(self):
            i = self.i
            for copy in self.z_back:
                copy.wait()
            for k in range(nz):
                flat_buf[i, k * chunk : (k + 1) * chunk] = zall[i, k].astype(F32)
            xout[i] = flat_buf[i].astype(BF16).reshape(9, part, C)
            for copy in farthest_first(self.x_back):
                copy.start()
            self.over[0].start()
            xall[i, x] = xout[i]

        def gather_core(self):
            for d in sorted(range(1, nx), key=lambda d: min(d, nx - d)):
                self.x_back[d - 1].wait()
                self.over[d].start()

        def finish(self):
            i = self.i
            base = core * HALF
            for k in range(nx):
                at = pl.ds(pl.multiple_of(base + k * part, part), part)
                gs_ref[i, :, at] = xall[i, k]
            base = HALF - base
            for copy in self.over:
                copy.wait()
            for k in range(nx):
                at = pl.ds(pl.multiple_of(base + k * part, part), part)
                gs_ref[i, :, at] = other[i, k]

    first = Reduction(0)
    second = Reduction(1)

    x_rim.start_up()
    x_rim.start_down()

    @pl.when(jnp.logical_not(encoder))
    def _():
        g_rim.start_up()
        g_rim.start_down()

    def clear(ref, width, top):
        @pl.when(first_row)
        def _():
            ref[0:width] = jnp.zeros((width, W, C), BF16)

        @pl.when(last_row)
        def _():
            ref[top - width : top] = jnp.zeros((width, W, C), BF16)

    for load in loads:
        load.wait()
    x_rim.wait()
    clear(xpad, 2, 8)
    fpre[...] = convolve(xpad[...], conv_matrix(a_ref), False)

    @pl.when(encoder)
    def _():
        hpad[...] = silu(fpre[...]).astype(BF16).reshape(6, W, C)
        clear(hpad, 1, 6)
        matrix = conv_matrix(b_ref)
        for h in (0, 2):
            pre = convolve(hpad[h : h + 4], matrix, False)
            stage[h : h + 2] = silu(pre).astype(BF16).reshape(2, W, C)
            skip_copies[h // 2].start()
            epre[h * W : (h + 2) * W] = pre
        out_ref[...] = stage[...]
        for copy in skip_copies:
            copy.wait_send()
        for copy in back_copies:
            copy.wait_recv()
        total = gpad[1:5].astype(F32) + back[...].astype(F32)
        spad[2:6] = (total * slope(epre[...]).reshape(4, W, C)).astype(BF16)
        s_rim.start_up()
        s_rim.start_down()
        weight_grad(hpad[...], spad[2:6], mine, 1)
        second.swap()
        s_rim.wait()
        clear(spad, 2, 8)
        second.reduce_x()
        hidden_back = convolve(spad[...], transpose_matrix(b_ref), True)
        dpad[...] = (hidden_back * slope(fpre[...])).astype(BF16).reshape(6, W, C)
        clear(dpad, 1, 6)

    @pl.when(jnp.logical_not(encoder))
    def _():
        skip_copies[0].wait_recv()
        s_rim.start_up()
        skip_copies[1].wait_recv()
        s_rim.start_down()
        g_rim.wait()
        s_rim.wait()
        clear(spad, 2, 8)
        fpre[...] += convolve(spad[...], conv_matrix(b_ref), False)
        pre = fpre[...]
        dpad[...] = (gpad[...].astype(F32) * slope(pre).reshape(6, W, C)).astype(BF16)
        clear(dpad, 1, 6)
        matrix = transpose_matrix(b_ref)
        for h in (0, 2):
            skip_grad = convolve(dpad[h : h + 4], matrix, True)
            stage[h : h + 2] = skip_grad.astype(BF16).reshape(2, W, C)
            back_copies[h // 2].start()
        out_ref[...] = silu(fpre[W : 5 * W]).astype(BF16).reshape(4, W, C)
        weight_grad(spad[1:7], dpad[1:5], mine, 1)
        second.swap()
        for copy in back_copies:
            copy.wait_send()
        second.reduce_x()

    weight_grad(xpad[1:7], dpad[1:5], mine, 0)

    first.swap()
    second.reduce_z()
    first.reduce_x()
    store_out = pltpu.make_async_copy(out_ref, out_hbm.at[0], local.at[4])
    store_out.start()
    ig_ref[...] = convolve(dpad[...], transpose_matrix(a_ref), True).astype(BF16).reshape(4, W, C)
    store_ig = pltpu.make_async_copy(ig_ref, ig_hbm.at[0], local.at[5])
    store_ig.start()
    first.reduce_z()
    second.gather_z()
    first.gather_z()
    second.gather_x()
    first.gather_x()
    second.gather_core()
    first.gather_core()
    second.finish()
    store_second = pltpu.make_async_copy(gs_ref.at[1], gs_hbm.at[1], local.at[6])
    store_second.start()
    first.finish()
    store_first = pltpu.make_async_copy(gs_ref.at[0], gs_hbm.at[0], local.at[7])
    store_first.start()
    for store in (store_out, store_ig, store_second, store_first):
        store.wait()


def farthest_first(copies):
    count = len(copies) + 1
    return [copies[d - 1] for d in sorted(range(1, count), key=lambda d: -min(d, count - d))]


def finish_kernel(
    factor, out_in, ig_in, gs_in, out_hbm, ig_hbm, first_hbm, second_hbm,
    out_ref, ig_ref, gs_ref, first, second, loaded, stored,
):
    loads = [
        pltpu.make_async_copy(src, dst, loaded.at[k])
        for k, (src, dst) in enumerate(
            [
                (gs_in.at[0], gs_ref.at[0]),
                (gs_in.at[1], gs_ref.at[1]),
                (out_in, out_ref),
                (ig_in, ig_ref),
            ]
        )
    ]
    stores = [
        pltpu.make_async_copy(src, dst, stored.at[k])
        for k, (src, dst) in enumerate(
            [(first, first_hbm), (second, second_hbm), (out_ref, out_hbm), (ig_ref, ig_hbm)]
        )
    ]
    for load in loads:
        load.start()
    for k, sums in enumerate((first, second)):
        loads[k].wait()
        sums[...] = (gs_ref[k].astype(F32) * factor).reshape(1, 3, 3, C, C)
        stores[k].start()
    for k in (2, 3):
        loads[k].wait()
        stores[k].start()
    for store in stores:
        store.wait()


def body(nx, nz, segments, incoming, cotangent, main_weight, second_weight):
    part = HALF // nx
    chunk = 9 * part // nz
    field = (1, STRIP, W, C)
    copies = 10 + 2 * (1 + 2 * (nx - 1) + 2 * (nz - 1) + nx)
    hbm = pl.BlockSpec(memory_space=pltpu.HBM)
    output, input_grad, sums = pl.pallas_call(
        functools.partial(kernel, nx, nz, segments),
        out_shape=(
            jax.ShapeDtypeStruct(field, BF16),
            jax.ShapeDtypeStruct(field, BF16),
            jax.ShapeDtypeStruct((2, 9, C, C), BF16),
        ),
        in_specs=[hbm] * 4,
        out_specs=(hbm,) * 3,
        scratch_shapes=[
            pltpu.VMEM((STRIP, W, C), BF16),
            pltpu.VMEM((STRIP, W, C), BF16),
            pltpu.VMEM((2, 9, C, C), BF16),
            pltpu.VMEM((8, W, C), BF16),
            pltpu.VMEM((8, W, C), BF16),
            pltpu.VMEM((6, W, C), BF16),
            pltpu.VMEM((6, W, C), BF16),
            pltpu.VMEM((6, W, C), BF16),
            pltpu.VMEM((1, 3, 3, C, C), BF16),
            pltpu.VMEM((1, 3, 3, C, C), BF16),
            pltpu.VMEM((6 * W, C), F32),
            pltpu.VMEM((4 * W, C), F32),
            pltpu.VMEM((4, W, C), BF16),
            pltpu.VMEM((4, W, C), BF16),
            pltpu.VMEM((2, CORES, 9, HALF, C), BF16),
            pltpu.VMEM((2, 9, HALF, C), BF16),
            pltpu.VMEM((2, nx, 9, part, C), BF16),
            pltpu.VMEM((2, nx - 1, 9, part, C), BF16),
            pltpu.VMEM((2, 9 * part, C), F32),
            pltpu.VMEM((2, nz, chunk, C), BF16),
            pltpu.VMEM((2, nz - 1, chunk, C), BF16),
            pltpu.VMEM((2, chunk, C), BF16),
            pltpu.VMEM((2, nz, chunk, C), BF16),
            pltpu.VMEM((2, 9, part, C), BF16),
            pltpu.VMEM((2, nx, 9, part, C), BF16),
            pltpu.VMEM((2, nx, 9, part, C), BF16),
            pltpu.SemaphoreType.DMA((8,)),
            pltpu.SemaphoreType.DMA((copies,)),
            pltpu.SemaphoreType.DMA((copies,)),
        ],
        compiler_params=pltpu.CompilerParams(
            collective_id=0, has_side_effects=True, vmem_limit_bytes=VMEM_BYTES
        ),
    )(incoming, cotangent, main_weight, second_weight)
    factor = 1.0 / math.sqrt(STRIP * nx * nz * CORES * W)
    weight = (1, 3, 3, C, C)
    return pl.pallas_call(
        functools.partial(finish_kernel, factor),
        out_shape=(
            jax.ShapeDtypeStruct(field, BF16),
            jax.ShapeDtypeStruct(field, BF16),
            jax.ShapeDtypeStruct(weight, F32),
            jax.ShapeDtypeStruct(weight, F32),
        ),
        in_specs=[hbm] * 3,
        out_specs=(hbm,) * 4,
        scratch_shapes=[
            pltpu.VMEM(field, BF16),
            pltpu.VMEM(field, BF16),
            pltpu.VMEM((2, 9, C, C), BF16),
            pltpu.VMEM(weight, F32),
            pltpu.VMEM(weight, F32),
            pltpu.SemaphoreType.DMA((4,)),
            pltpu.SemaphoreType.DMA((4,)),
        ],
        compiler_params=pltpu.CompilerParams(vmem_limit_bytes=VMEM_BYTES),
    )(output, input_grad, sums)


def build(mesh, nz):
    segments = mesh.shape["segment"]
    nx = mesh.shape["rows"] // (nz * CORES)
    field = P("segment", "rows", None, None)
    weight = P("segment", None, None, None, None)
    return jax.shard_map(
        functools.partial(body, nx, nz, segments),
        mesh=mesh,
        in_specs=(field, field, weight, weight),
        out_specs=(field, field, weight, weight),
        check_vma=False,
    )


def solution(mesh):
    return build(mesh, Z_SIZE)
```
